32 devices in a mesh: dp: 8 (over z, y), seq: 4 (over x, core).
Axes of the slice: x: 2, y: 2, z: 4, core: 2. Of those that a mesh axis runs over, the one named last changes fastest.
Arguments:
- tokens: bfloat16 [8, 512, 1024], P('dp', 'seq'), may hold values from -6 to 6
- cache_keys: bfloat16 [8, 2048, 1024], P('dp', 'seq')
- cache_values: bfloat16 [8, 2048, 1024], P('dp', 'seq'), may hold values from -6 to 6
- qkv_weight: bfloat16 [1024, 3072], P(None, 'seq'), may hold values from -0.1875 to 0.1875
- qkv_bias: float32 [3072], replicated, may hold values from -3 to 3
- out_weight: bfloat16 [1024, 1024], P('seq', 'dp'), may hold values from -0.1875 to 0.1875
- out_bias: float32 [1024], replicated, may hold values from -3 to 3
- norm_gain: float32 [1024], replicated, may hold values from 0.1 to 1.9
- norm_bias: float32 [1024], replicated, may hold values from -3 to 3
- cached_len: int32 [8], replicated, may hold values from 0 to 2048, as said below
- span_len: int32 [8], replicated, may hold values from 1 to 512, as said below
- slot_request: int32 [8], replicated, may hold values from 0 to 7, each once
Outputs:
- normed: bfloat16 [8, 512, 1024], P('dp', 'seq')
The draws below stay inside these ranges and needn't reach their ends.
Inputs may be any that keep to these rules, and one draw needn't show every extreme that they name: `cached_len`: some request has exactly 2048 cached positions. `span_len`: some request has exactly 512 new tokens in use. `slot_request`: each request names one slot.
All inputs are finite; a program needn't handle non-finite values.
Results may differ from the reference program's by a relative error of at most 0.0085.
Values may be sent and summed in bfloat16 or wider, within the bound.
A program may use at most 64 MiB of HBM per device.

```python
import jax
import jax.numpy as jnp
from jax import lax

D = 1024
HEADS = 16
HEAD_DIM = 64
SPAN_DEV = 128
CACHE_DEV = 512
SPAN = 512
CACHE = 2048
REQUESTS = 8
N_SEQ = 4


def draw_cache_keys(key, part):
    shape = (REQUESTS, CACHE, D)
    return jax.random.normal(key, shape, jnp.float32).astype(jnp.bfloat16)


def draw_cached_len(key, part):
    first, second, third = jax.random.split(jax.random.fold_in(key, 11), 3)
    ranking = jax.random.permutation(first, REQUESTS)
    many = max(1, REQUESTS // 8)
    shorter = jax.random.randint(second, (REQUESTS,), 0, max(2, CACHE // 4))
    longer = CACHE - jax.random.randint(third, (REQUESTS,), 0, max(2, CACHE // 16))
    result = jnp.where(ranking < many, longer, shorter)
    return jnp.where(ranking == 0, CACHE, result).astype(jnp.int32)


def draw_span_len(key, part):
    first, second = jax.random.split(jax.random.fold_in(key, 23), 2)
    ranking = jax.random.permutation(first, REQUESTS)
    drawn = jax.random.randint(second, (REQUESTS,), SPAN // 4, SPAN + 1)
    return jnp.where(ranking == 0, SPAN, drawn).astype(jnp.int32)


def levels(stream_key, extent, shards, low, largest):
    factor_of = 1.0
    for axis_at, blocks in shards:
        heights = jax.random.uniform(jax.random.fold_in(jax.random.fold_in(stream_key, 6), axis_at), (blocks,), jnp.float32, low / len(shards), largest / len(shards))
        factor_of = factor_of * jnp.repeat(jnp.exp(heights), extent[axis_at] // blocks).reshape((-1,) + (1,) * (len(extent) - 1 - axis_at))
    return factor_of


def noise(rng, shape, scale, bound, shards=(), dtype=jnp.bfloat16):
    values = jax.random.normal(rng, shape, jnp.float32) * scale
    if len(shards) > 0:
        values = levels(rng, shape, shards, -0.22, 0.18) * values
    return jnp.clip(values, min=-bound, max=bound).astype(dtype)


def setup_inputs(seed: int = 0) -> dict:
    splits = jax.random.split(jax.random.key(seed), 13)
    return {
        "tokens": noise(splits[0], (REQUESTS, SPAN, D), 1.0, 6.0, ((0, 8), (1, 4))),
        "cache_keys": draw_cache_keys(jax.random.fold_in(splits[12], 71), 0),
        "cache_values": noise(splits[2], (REQUESTS, CACHE, D), 1.0, 6.0, ((0, 8), (1, 4))),
        "qkv_weight": noise(splits[3], (D, 3 * D), D ** -0.5, 0.1875, ((1, 4),)),
        "qkv_bias": noise(splits[4], (3 * D,), 0.5, 3.0, (), jnp.float32),
        "out_weight": noise(splits[5], (D, D), D ** -0.5, 0.1875, ((0, 4), (1, 8))),
        "out_bias": noise(splits[6], (D,), 0.5, 3.0, (), jnp.float32),
        "norm_gain": jnp.clip(1.0 + 0.18 * jax.random.normal(splits[7], (D,), jnp.float32), 0.1, 1.9),
        "norm_bias": noise(splits[8], (D,), 0.5, 3.0, (), jnp.float32),
        "cached_len": draw_cached_len(jax.random.fold_in(splits[12], 71), 0),
        "span_len": draw_span_len(jax.random.fold_in(splits[12], 71), 0),
        "slot_request": jax.random.permutation(splits[11], REQUESTS).astype(jnp.int32),
    }


neg_big = -1e+30

def reference(tokens, cache_keys, cache_values, qkv_weight, qkv_bias, out_weight, out_bias, norm_gain, norm_bias, cached_len, span_len, slot_request):
    scale = HEAD_DIM ** (-0.5)

    def one_slot(index):
        request = slot_request[index]
        cached = cached_len[request]
        filled = span_len[request]
        inputs = tokens[index]
        projected = (jnp.dot(inputs, qkv_weight, preferred_element_type=jnp.float32) + qkv_bias).astype(jnp.bfloat16)
        projected = projected.reshape(SPAN, HEADS, 3, HEAD_DIM)
        queries = projected[:, :, 0]
        new_keys = projected[:, :, 1]
        new_values = projected[:, :, 2]
        keys_all = cache_keys[index].reshape(CACHE, HEADS, HEAD_DIM)
        values_all = cache_values[index].reshape(CACHE, HEADS, HEAD_DIM)
        positions = jnp.arange(SPAN)
        parts = []
        for group in range(N_SEQ):
            keys = jnp.concatenate([keys_all[group * CACHE_DEV:(group + 1) * CACHE_DEV], new_keys[group * SPAN_DEV:(group + 1) * SPAN_DEV]], 0)
            values = jnp.concatenate([values_all[group * CACHE_DEV:(group + 1) * CACHE_DEV], new_values[group * SPAN_DEV:(group + 1) * SPAN_DEV]], 0)
            cache_pos = group * CACHE_DEV + jnp.arange(CACHE_DEV)
            new_pos = group * SPAN_DEV + jnp.arange(SPAN_DEV)
            live_cache = jnp.broadcast_to(cache_pos[None, :] < cached, (SPAN, CACHE_DEV))
            live_new = (new_pos[None, :] <= positions[:, None]) & (new_pos[None, :] < filled)
            live = jnp.concatenate([live_cache, live_new], 1)
            scores = jnp.einsum('thd,khd->htk', queries.astype(jnp.float32), keys.astype(jnp.float32)) * scale
            masked = jnp.where(live[None], scores, neg_big)
            top = lax.optimization_barrier(jnp.max(masked, axis=2))
            weights = jnp.where(live[None], jnp.exp(masked - top[:, :, None]), 0.0)
            total = lax.optimization_barrier(jnp.sum(weights, axis=2))
            weights_b = lax.optimization_barrier(weights.astype(jnp.bfloat16))
            numer = jnp.einsum('htk,khd->thd', weights_b.astype(jnp.float32), values.astype(jnp.float32))
            own = (numer / jnp.maximum(total, 1.0).T[:, :, None]).astype(jnp.bfloat16)
            own = lax.optimization_barrier(own)
            parts.append((own.astype(jnp.float32), top.T, total.T))
        best = parts[0][1]
        for part in parts[1:]:
            best = jnp.maximum(best, part[1])
        summed = jnp.zeros((SPAN, HEADS, HEAD_DIM), jnp.float32)
        denom = jnp.zeros((SPAN, HEADS), jnp.float32)
        for own, top, total in parts:
            share = total * jnp.exp(top - best)
            summed = summed + share[:, :, None] * own
            denom = denom + share
        attn = (summed / denom[:, :, None]).reshape(SPAN, D).astype(jnp.bfloat16)
        mixed = jnp.dot(attn, out_weight, preferred_element_type=jnp.float32) + out_bias + inputs.astype(jnp.float32)
        center = mixed - lax.optimization_barrier(jnp.mean(mixed, axis=1, keepdims=True))
        spread = lax.optimization_barrier(jnp.mean(center * center, axis=1, keepdims=True))
        return (center * lax.rsqrt(spread + 1e-05) * norm_gain + norm_bias).astype(jnp.bfloat16)
    return lax.map(one_slot, jnp.arange(REQUESTS))
```

```python
import functools

import jax
import jax.numpy as jnp
from jax import lax
from jax.experimental import pallas as pl
from jax.experimental.pallas import tpu as pltpu
from jax.sharding import PartitionSpec as P

HEAD_DIM = 64
LANES = 128
LIVE = 3e38
DEAD = -1e30
F32 = jnp.float32
BF16 = jnp.bfloat16
MESH = pl.DeviceIdType.MESH
LEADER = 1
DP = 8
ROW = 2


def peers():
    me = lax.axis_index("seq")
    core = me % 2
    partner = me + 1 - 2 * core
    twin = (me + 2) % 4
    diag = (partner + 2) % 4
    return me, core, partner, twin, diag


def cols(index, width):
    return pl.ds(pl.multiple_of(index * width, 128), width)


def rows_of(index, height):
    return pl.ds(pl.multiple_of(index * height, 128), height)


def nt(a, b):
    return lax.dot_general(a, b, (((1,), (1,)), ((), ())), preferred_element_type=F32)


def lanes(rows):
    return lax.broadcasted_iota(jnp.int32, (rows, LANES), 1)


def split(pair, even, odd):
    low = lanes(pair.shape[0]) < HEAD_DIM
    return jnp.where(low, pair, even), jnp.where(low, odd, pair)


def attend(heads, query, keys, values, caps):
    def scores(h):
        out = []
        for k, cap in zip(keys, caps):
            s = nt(query(h), k(h))
            out.append(s if cap is None else jnp.minimum(s, cap))
        return out

    now = scores(0)
    tops, products = [], []
    for h in range(heads):
        later = scores(h + 1) if h + 1 < heads else None
        top = functools.reduce(jnp.maximum, [jnp.max(s, 1, keepdims=True) for s in now])
        product = 0.0
        for s, v in zip(now, values):
            product = product + jnp.dot(
                jnp.exp(s - top).astype(BF16), v(h), preferred_element_type=F32
            )
        tops.append(top)
        products.append(product)
        now = later
    return tops, products


def finish(tops, products, base):
    rows = products[0].shape[0]
    lane = lanes(rows)
    low = lane < HEAD_DIM
    parts = []
    left = jnp.zeros((rows, LANES), F32)
    right = jnp.zeros((rows, LANES), F32)
    for pair in range(len(products) // 2):
        a, b = products[2 * pair], products[2 * pair + 1]
        total = jnp.where(low, b, a)
        log = jnp.log(total)
        even, odd = base + 2 * pair, base + 2 * pair + 1
        right = jnp.where(lane == HEAD_DIM + even, tops[2 * pair] + log, right)
        left = jnp.where(lane == odd, tops[2 * pair + 1] + log, left)
        parts.append(jnp.where(low, a, b) / pltpu.roll(total, HEAD_DIM, 1))
    return parts, left + pltpu.roll(right, HEAD_DIM, 1)


def spread(tile, base, heads):
    rows = tile.shape[0]
    low = lanes(rows) < HEAD_DIM
    out = []
    for pair in range(heads // 2):
        at = base + 2 * pair
        out.append(jnp.where(low, tile[:, at : at + 1], tile[:, at + 1 : at + 2]))
    return jnp.concatenate(out, 1)


def kernel(
    gather,
    cached_ref,
    span_ref,
    slot_ref,
    tokens_hbm,
    keys_hbm,
    values_hbm,
    weight_hbm,
    out_weight_hbm,
    bias_ref,
    out_bias_ref,
    gain_ref,
    shift_ref,
    out_ref,
    tok,
    weight,
    kc,
    vc,
    k0,
    v0,
    k1,
    v1,
    q0,
    qo,
    qt,
    caps,
    keep,
    keep_stat,
    send_stat,
    part_send,
    part_recv,
    stat_send,
    stat_recv,
    mixed_send,
    mixed_recv,
    wo,
    local_sem,
    tok_send,
    tok_recv,
    cache_send,
    cache_recv,
    q_send,
    q_recv,
    p_send,
    p_recv,
    s_sem,
    m_sem,
    x_sem,
    w_send,
    w_recv,
    ready,
    far_ready,
):
    me, core, partner, twin, diag = peers()
    chip = me // 2
    rows = tok.shape[1]
    half = 2 * rows
    cache_rows = kc.shape[2]
    old = 2 * cache_rows
    width = kc.shape[3]
    heads = width // HEAD_DIM
    dp = lax.axis_index("dp")
    request = slot_ref[dp]
    cached = cached_ref[request]
    filled = span_ref[request]
    new_rows = tok.shape[0] * rows

    locals_ = [
        pltpu.make_async_copy(tokens_hbm.at[0], tok.at[me], local_sem.at[0]),
        pltpu.make_async_copy(weight_hbm, weight, local_sem.at[1]),
    ]
    for group, owner in enumerate((me, twin)):
        for at, (hbm, buf) in enumerate(((keys_hbm, kc), (values_hbm, vc))):
            locals_.append(
                pltpu.make_async_copy(
                    hbm.at[0, :, cols(owner, width)],
                    buf.at[group, core],
                    local_sem.at[2 + 2 * group + at],
                )
            )
    if gather:
        piece = out_weight_hbm.shape[1]
        out_copies = [
            pltpu.make_async_copy(out_weight_hbm, wo.at[0, :, cols(dp, piece)], local_sem.at[6])
        ]
    else:
        out_copies = [
            pltpu.make_async_copy(out_weight_hbm.at[owner], wo.at[at], local_sem.at[6 + at])
            for at, owner in enumerate((me, twin))
        ]
    for copy in locals_ + out_copies:
        copy.start()

    def remote(src, dst, send, recv, device):
        return pltpu.make_async_remote_copy(
            src_ref=src,
            dst_ref=dst,
            send_sem=send,
            recv_sem=recv,
            device_id=device,
            device_id_type=MESH,
        )

    def near(src, dst, send, recv, index):
        return remote(src, dst, send, recv, {"seq": index})

    to_twin = near(tokens_hbm.at[0], tok.at[me], tok_send.at[1], tok_recv.at[1], twin)
    to_partner = near(tokens_hbm.at[0], tok.at[me], tok_send.at[0], tok_recv.at[0], partner)
    forward = near(tok.at[twin], tok.at[twin], tok_send.at[2], tok_recv.at[2], partner)
    cache_copies = []
    for group, owner in enumerate((partner, diag)):
        for at, (hbm, buf) in enumerate(((keys_hbm, kc), (values_hbm, vc))):
            cache_copies.append(
                near(
                    hbm.at[0, :, cols(owner, width)],
                    buf.at[group, core],
                    cache_send.at[2 * group + at],
                    cache_recv.at[2 * group + at],
                    partner,
                )
            )
    far_peers = []
    if gather:
        weight_twin = near(
            out_weight_hbm, wo.at[1, :, cols(dp, piece)], x_sem.at[0], x_sem.at[1], twin
        )
        side = dp + 1 - 2 * (dp % ROW)
        far_peers = [(dp + ROW * k) % DP for k in range(1, DP // ROW)] + [side]

        def direct(part, k):
            at = wo.at[part, :, cols(dp, piece)]
            return remote(at, at, w_send.at[part, k], w_recv.at[part, k], {"dp": far_peers[k]})

        def pass_on(part, k):
            origin = (dp + DP - ROW * (k + 1)) % DP
            at = wo.at[part, :, cols(origin, piece)]
            slot = len(far_peers) + k
            return remote(at, at, w_send.at[part, slot], w_recv.at[part, slot], {"dp": side})

    barrier = pltpu.get_barrier_semaphore()

    def tell(sem, index):
        pl.semaphore_signal(sem, inc=1, device_id={"seq": index}, device_id_type=MESH)

    @pl.when(me == 1)
    def _():
        tell(barrier, 0)
        tell(barrier, 3)

    @pl.when(me == 3)
    def _():
        tell(barrier, 2)

    @pl.when(me != 1)
    def _():
        pl.semaphore_wait(barrier, 1 + (me == 2).astype(jnp.int32))

    @pl.when(me == 0)
    def _():
        tell(barrier, 2)
        tell(ready.at[0], 1)

    @pl.when(me == 2)
    def _():
        tell(ready.at[2], 0)
        tell(ready.at[2], 1)
        tell(ready.at[2], 3)

    @pl.when(me == 3)
    def _():
        tell(ready.at[3], 1)

    def cross():
        if gather:
            weight_twin.start()
        to_twin.start()

    @pl.when(chip == 1)
    def _():
        cross()

    @pl.when(me == 1)
    def _():
        pl.semaphore_wait(ready.at[0], 1)

    @pl.when(me == 3)
    def _():
        pl.semaphore_wait(ready.at[2], 1)

    to_partner.start()
    for copy in cache_copies:
        copy.start()

    @pl.when(me == 0)
    def _():
        pl.semaphore_wait(ready.at[2], 1)

    @pl.when(me == 1)
    def _():
        pl.semaphore_wait(ready.at[3], 1)

    @pl.when(chip == 0)
    def _():
        cross()

    @pl.when(me == LEADER)
    def _():
        pl.semaphore_wait(ready.at[2], 1)
        for peer in far_peers:
            pl.semaphore_signal(barrier, inc=1, device_id={"dp": peer}, device_id_type=MESH)

    def far_start():
        @pl.when(me == LEADER)
        def _():
            pl.semaphore_wait(barrier, len(far_peers))
            for index in (0, 2, 3):
                tell(far_ready, index)

        @pl.when(me != LEADER)
        def _():
            pl.semaphore_wait(far_ready, 1)

        out_copies[0].wait()
        for k in range(len(far_peers)):
            direct(0, k).start()
        weight_twin.wait_recv()
        for k in range(len(far_peers)):
            direct(1, k).start()

    bias = bias_ref[:, cols(me, 3 * width)]
    low = lanes(half) < HEAD_DIM
    lane = lanes(half)
    ones = jnp.ones((half, LANES), BF16)
    none = jnp.zeros((half, LANES), BF16)
    first = jnp.where(lane == 0, 1.0, 0.0).astype(BF16)
    middle = jnp.where(lane == HEAD_DIM, 1.0, 0.0).astype(BF16)

    def project(side_):
        inputs = tok[pl.ds(2 * side_, 2)].reshape(half, tok.shape[2])
        at = pl.ds(pl.multiple_of(old + side_ * half, 128), half)
        for pair in range(heads // 2):
            here = slice(6 * pair * HEAD_DIM, 6 * (pair + 1) * HEAD_DIM)
            summed = jnp.dot(inputs, weight[:, here], preferred_element_type=F32) + bias[:, here]
            a, b, c = (summed[:, i * LANES : (i + 1) * LANES] for i in range(3))
            query = (jnp.where(low, a, b).astype(BF16).astype(F32) * HEAD_DIM**-0.5).astype(BF16)
            key = pltpu.roll(jnp.where(low, c, a), HEAD_DIM, 1).astype(BF16)
            value = jnp.where(low, b, c).astype(BF16)
            qo[side_, :, pair * LANES : (pair + 1) * LANES] = query
            q0[side_, 2 * pair], q0[side_, 2 * pair + 1] = split(query, middle, first)
            k0[2 * pair, at], k0[2 * pair + 1, at] = split(key, none, none)
            v0[2 * pair, at], v0[2 * pair + 1, at] = split(value, ones, ones)

    def query_copy(side_):
        return near(qo.at[side_], qt.at[side_], q_send.at[side_], q_recv.at[side_], twin)

    def prepare(group, keys, values):
        lane_ = lanes(cache_rows)
        for c in range(2):
            place = lax.broadcasted_iota(jnp.int32, (cache_rows, LANES), 0)
            live = (2 * chip + c) * cache_rows + place < cached
            scale = jnp.where(live, 1.0, 0.0).astype(BF16)
            cap = jnp.where(live, 0.0, DEAD)
            cap_even = jnp.where(lane_ == HEAD_DIM, cap, 0.0).astype(BF16)
            cap_odd = jnp.where(lane_ == 0, cap, 0.0).astype(BF16)
            full = jnp.ones((cache_rows, LANES), BF16)
            at = slice(c * cache_rows, (c + 1) * cache_rows)
            for pair in range(heads // 2):
                here = slice(pair * LANES, (pair + 1) * LANES)
                key = kc[group, c, :, here] * scale
                keys[2 * pair, at], keys[2 * pair + 1, at] = split(key, cap_even, cap_odd)
                value = vc[group, c, :, here]
                values[2 * pair, at], values[2 * pair + 1, at] = split(value, full, full)

    def own_heads(side_, base):
        tops, products = attend(
            heads,
            lambda h: q0[side_, h],
            [lambda h: k0[h, 0:old], lambda h: k0[h, old : old + new_rows]],
            [lambda h: v0[h, 0:old], lambda h: v0[h, old : old + new_rows]],
            [None, caps[side_]],
        )
        return finish(tops, products, base)

    def twin_heads(side_, base):
        queries = []
        for pair in range(heads // 2):
            queries.extend(split(qt[side_, :, pair * LANES : (pair + 1) * LANES], middle, first))
        tops, products = attend(
            heads,
            lambda h: queries[h],
            [lambda h: k1[h]],
            [lambda h: v1[h]],
            [None],
        )
        return finish(tops, products, base)

    def part_copy(group, block):
        return near(
            part_send.at[group, block],
            part_recv.at[1 - group, block],
            p_send.at[group, block],
            p_recv.at[1 - group, block],
            twin,
        )

    stat_copy = near(stat_send, stat_recv, s_sem.at[0], s_sem.at[1], twin)

    locals_[0].wait()
    locals_[1].wait()
    to_partner.wait_recv()
    project(chip)
    if gather:

        @pl.when(dp >= DP // 2)
        def _():
            far_start()

    for side_ in range(2):
        row = side_ * half + lax.broadcasted_iota(jnp.int32, (half, new_rows), 0)
        new = lax.broadcasted_iota(jnp.int32, (half, new_rows), 1)
        caps[side_] = jnp.where((new <= row) & (new < filled), LIVE, DEAD)
    for at in (0, 1):
        locals_[2 + at].wait()
        cache_copies[at].wait_recv()
    prepare(0, k0, v0)
    to_twin.wait_send()
    query_copy(chip).start()
    for at in (2, 3):
        locals_[2 + at].wait()
        cache_copies[at].wait_recv()
    prepare(1, k1, v1)
    if gather:

        @pl.when(dp < DP // 2)
        def _():
            far_start()

    to_twin.wait_recv()
    forward.start()
    forward.wait_recv()
    project(1 - chip)
    query_copy(1 - chip).start()

    def send_part(group, parts):
        for pair in range(heads // 2):
            both = parts[pair].astype(BF16)
            for block in range(2):
                part_send[group, block, :, pair * LANES : (pair + 1) * LANES] = both[
                    block * rows : (block + 1) * rows
                ]
        for block in (1 - core, core):
            part_copy(group, block).start()

    def keep_part(group, parts):
        for pair in range(heads // 2):
            for block in range(2):
                at = group * width + pair * LANES
                keep[block, :, at : at + LANES] = parts[pair][block * rows : (block + 1) * rows]

    parts, stat = own_heads(1 - chip, heads)
    send_part(0, parts)
    send_stat[...] = stat
    if gather:
        for k in range(len(far_peers) - 1):
            direct(0, k).wait_recv()
            pass_on(0, k).start()

    query_copy(1 - chip).wait_recv()
    parts, stat = twin_heads(1 - chip, 0)
    send_part(1, parts)
    stat = stat + send_stat[...]
    for block in range(2):
        stat_send[:, block * rows : (block + 1) * rows] = stat[
            block * rows : (block + 1) * rows
        ].T[0 : 2 * heads]
    stat_copy.start()
    if gather:
        for k in range(len(far_peers) - 1):
            direct(1, k).wait_recv()
            pass_on(1, k).start()

    parts, stat = own_heads(chip, 0)
    keep_part(0, parts)
    keep_stat[...] = stat.reshape(2, rows, LANES)
    query_copy(chip).wait_recv()
    parts, stat = twin_heads(chip, heads)
    keep_part(1, parts)
    keep_stat[...] = keep_stat[...] + stat.reshape(2, rows, LANES)

    for copy in out_copies if not gather else []:
        copy.wait()
    if gather:
        for part in range(2):
            direct(part, len(far_peers) - 1).wait_recv()
            for k in range(len(far_peers) - 1):
                pass_on(part, k).wait_recv()

    stat_copy.wait_recv()

    def combine(block):
        for group in range(2):
            part_copy(1 - group, block).wait_recv()
        other = jnp.concatenate(
            [
                stat_recv[:, cols(block, rows)],
                jnp.zeros((rows - 2 * heads, rows), F32),
            ],
            0,
        ).T
        share = 1.0 / (1.0 + jnp.exp(other - keep_stat[block]))
        total = 0.0
        for group in range(2):
            at = slice(group * width, (group + 1) * width)
            theirs = part_recv[group, block].astype(F32)
            attn = theirs + spread(share, group * heads, heads) * (keep[block, :, at] - theirs)
            total = total + jnp.dot(attn.astype(BF16), wo[group], preferred_element_type=F32)
        return total

    mixed_copy = near(mixed_send, mixed_recv, m_sem.at[0], m_sem.at[1], partner)
    mixed_send[...] = combine(1 - core).astype(BF16)
    mixed_copy.start()
    mixed = combine(core) + out_bias_ref[...] + tok[me].astype(F32)
    mixed_copy.wait_recv()
    mixed = mixed + mixed_recv[...].astype(F32)
    center = mixed - jnp.mean(mixed, axis=1, keepdims=True)
    variance = jnp.mean(center * center, axis=1, keepdims=True)
    normed = center * lax.rsqrt(variance + 1e-05) * gain_ref[...] + shift_ref[...]
    out_ref[0] = normed.astype(BF16)

    sent = [to_partner, forward, stat_copy, mixed_copy] + cache_copies
    sent += [query_copy(s) for s in range(2)]
    sent += [part_copy(g, b) for g in range(2) for b in range(2)]
    if gather:
        sent.append(weight_twin)
        for part in range(2):
            sent += [direct(part, k) for k in range(len(far_peers))]
            sent += [pass_on(part, k) for k in range(len(far_peers) - 1)]
    for copy in sent:
        copy.wait_send()


def local(
    tokens,
    cache_keys,
    cache_values,
    qkv_weight,
    qkv_bias,
    out_weight,
    out_bias,
    norm_gain,
    norm_bias,
    cached_len,
    span_len,
    slot_request,
):
    rows, model = tokens.shape[1:]
    cache_rows = cache_keys.shape[1]
    width = qkv_weight.shape[1] // 3
    heads = width // HEAD_DIM
    blocks = lax.axis_size("seq")
    half = 2 * rows
    old = 2 * cache_rows
    total = old + blocks * rows
    hbm = pl.BlockSpec(memory_space=pltpu.HBM)
    vmem = pl.BlockSpec(memory_space=pltpu.VMEM)
    smem = pl.BlockSpec(memory_space=pltpu.SMEM)
    dma = pltpu.SemaphoreType.DMA

    gather = lax.axis_size("dp") == DP and out_weight.shape[1] % 128 == 0
    if not gather:
        out_weight = lax.all_gather(out_weight, "dp", axis=1, tiled=True)
        out_weight = lax.all_gather(out_weight, "seq", axis=0)

    return pl.pallas_call(
        functools.partial(kernel, gather),
        out_shape=jax.ShapeDtypeStruct((1, rows, model), BF16),
        in_specs=[smem] * 3 + [hbm] * 5 + [vmem] * 4,
        out_specs=vmem,
        scratch_shapes=[
            pltpu.VMEM((blocks, rows, model), BF16),
            pltpu.VMEM((model, 3 * width), BF16),
            pltpu.VMEM((2, 2, cache_rows, width), BF16),
            pltpu.VMEM((2, 2, cache_rows, width), BF16),
            pltpu.VMEM((heads, total, LANES), BF16),
            pltpu.VMEM((heads, total, LANES), BF16),
            pltpu.VMEM((heads, old, LANES), BF16),
            pltpu.VMEM((heads, old, LANES), BF16),
            pltpu.VMEM((2, heads, half, LANES), BF16),
            pltpu.VMEM((2, half, width), BF16),
            pltpu.VMEM((2, half, width), BF16),
            pltpu.VMEM((2, half, blocks * rows), F32),
            pltpu.VMEM((2, rows, 2 * width), F32),
            pltpu.VMEM((2, rows, LANES), F32),
            pltpu.VMEM((half, LANES), F32),
            pltpu.VMEM((2, 2, rows, width), BF16),
            pltpu.VMEM((2, 2, rows, width), BF16),
            pltpu.VMEM((2 * heads, half), F32),
            pltpu.VMEM((2 * heads, half), F32),
            pltpu.VMEM((rows, model), BF16),
            pltpu.VMEM((rows, model), BF16),
            pltpu.VMEM((2, width, model), BF16),
            dma((8,)),
            dma((3,)),
            dma((3,)),
            dma((4,)),
            dma((4,)),
            dma((2,)),
            dma((2,)),
            dma((2, 2)),
            dma((2, 2)),
            dma((2,)),
            dma((2,)),
            dma((2,)),
            dma((2, DP)),
            dma((2, DP)),
            pltpu.SemaphoreType.REGULAR((4,)),
            pltpu.SemaphoreType.REGULAR,
        ],
        compiler_params=pltpu.CompilerParams(
            collective_id=0, has_side_effects=True, vmem_limit_bytes=60 << 20
        ),
        cost_estimate=pl.CostEstimate(
            flops=6_000_000_000, bytes_accessed=6_000_000, transcendentals=5_000_000
        ),
        name="sublayer",
    )(
        cached_len,
        span_len,
        slot_request,
        tokens,
        cache_keys,
        cache_values,
        qkv_weight,
        out_weight,
        qkv_bias.reshape(1, -1),
        out_bias.reshape(1, -1),
        norm_gain.reshape(1, -1),
        norm_bias.reshape(1, -1),
    )


def solution(mesh):
    return jax.shard_map(
        local,
        mesh=mesh,
        in_specs=(
            P("dp", "seq", None),
            P("dp", "seq", None),
            P("dp", "seq", None),
            P(None, "seq"),
            P(),
            P("seq", "dp"),
            P(),
            P(),
            P(),
            P(),
            P(),
            P(),
        ),
        out_specs=P("dp", "seq", None),
        check_vma=False,
    )
```

```python
import functools

import jax
import jax.numpy as jnp
from jax import lax
from jax.experimental import pallas as pl
from jax.experimental.pallas import tpu as pltpu
from jax.sharding import PartitionSpec as P

HEAD_DIM = 64
LANES = 128
LIVE = 3e38
DEAD = -1e30
F32 = jnp.float32
BF16 = jnp.bfloat16
MESH = pl.DeviceIdType.MESH
LEADER = 1
DP = 8
ROW = 2
LINE = DP // ROW


def peers():
    me = lax.axis_index("seq")
    core = me % 2
    partner = me + 1 - 2 * core
    twin = (me + 2) % 4
    diag = (partner + 2) % 4
    return me, core, partner, twin, diag


def cols(index, width):
    return pl.ds(pl.multiple_of(index * width, 128), width)


def rows_of(index, height):
    return pl.ds(pl.multiple_of(index * height, 128), height)


def nt(a, b):
    return lax.dot_general(a, b, (((1,), (1,)), ((), ())), preferred_element_type=F32)


def lanes(rows):
    return lax.broadcasted_iota(jnp.int32, (rows, LANES), 1)


def split(pair, even, odd):
    low = lanes(pair.shape[0]) < HEAD_DIM
    return jnp.where(low, pair, even), jnp.where(low, odd, pair)


def attend(heads, query, keys, values, caps, between=()):
    def scores(h):
        out = []
        for k, cap in zip(keys, caps):
            s = nt(query(h), k(h))
            out.append(s if cap is None else jnp.minimum(s, cap))
        return out

    now = scores(0)
    tops, products = [], []
    for h in range(heads):
        later = scores(h + 1) if h + 1 < heads else None
        top = functools.reduce(jnp.maximum, [jnp.max(s, 1, keepdims=True) for s in now])
        product = 0.0
        for s, v in zip(now, values):
            product = product + jnp.dot(
                jnp.exp(s - top).astype(BF16), v(h), preferred_element_type=F32
            )
        tops.append(top)
        products.append(product)
        now = later
        if h < len(between):
            between[h]()
    return tops, products


def finish(tops, products, base):
    rows = products[0].shape[0]
    lane = lanes(rows)
    low = lane < HEAD_DIM
    parts = []
    left = jnp.zeros((rows, LANES), F32)
    right = jnp.zeros((rows, LANES), F32)
    for pair in range(len(products) // 2):
        a, b = products[2 * pair], products[2 * pair + 1]
        total = jnp.where(low, b, a)
        log = jnp.log(total)
        even, odd = base + 2 * pair, base + 2 * pair + 1
        right = jnp.where(lane == HEAD_DIM + even, tops[2 * pair] + log, right)
        left = jnp.where(lane == odd, tops[2 * pair + 1] + log, left)
        parts.append(jnp.where(low, a, b) / pltpu.roll(total, HEAD_DIM, 1))
    return parts, left + pltpu.roll(right, HEAD_DIM, 1)


def spread(tile, base, heads):
    rows = tile.shape[0]
    low = lanes(rows) < HEAD_DIM
    out = []
    for pair in range(heads // 2):
        at = base + 2 * pair
        out.append(jnp.where(low, tile[:, at : at + 1], tile[:, at + 1 : at + 2]))
    return jnp.concatenate(out, 1)


def kernel(
    gather,
    cached_ref,
    span_ref,
    slot_ref,
    tokens_hbm,
    keys_hbm,
    values_hbm,
    weight_hbm,
    out_weight_hbm,
    bias_ref,
    out_bias_ref,
    gain_ref,
    shift_ref,
    out_ref,
    tok,
    weight,
    kc,
    vc,
    k0,
    v0,
    k1,
    v1,
    q0,
    qo,
    qt,
    caps,
    keep,
    keep_stat,
    send_stat,
    part_send,
    part_recv,
    stat_send,
    stat_recv,
    mixed_send,
    mixed_recv,
    wo,
    local_sem,
    tok_send,
    tok_recv,
    cache_send,
    cache_recv,
    q_send,
    q_recv,
    p_send,
    p_recv,
    s_sem,
    m_sem,
    x_sem,
    w_send,
    w_recv,
    ready,
    up_sem,
    far_ready,
):
    me, core, partner, twin, diag = peers()
    chip = me // 2
    rows = tok.shape[1]
    half = 2 * rows
    cache_rows = kc.shape[2]
    old = 2 * cache_rows
    width = kc.shape[3]
    heads = width // HEAD_DIM
    dp = lax.axis_index("dp")
    request = slot_ref[dp]
    cached = cached_ref[request]
    filled = span_ref[request]
    new_rows = tok.shape[0] * rows

    locals_ = [
        pltpu.make_async_copy(tokens_hbm.at[0], tok.at[me], local_sem.at[0]),
        pltpu.make_async_copy(weight_hbm, weight, local_sem.at[1]),
    ]
    for group, owner in enumerate((me, twin)):
        for at, (hbm, buf) in enumerate(((keys_hbm, kc), (values_hbm, vc))):
            locals_.append(
                pltpu.make_async_copy(
                    hbm.at[0, :, cols(owner, width)],
                    buf.at[group, core],
                    local_sem.at[2 + 2 * group + at],
                )
            )
    if gather:
        piece = out_weight_hbm.shape[1]
        out_copies = [
            pltpu.make_async_copy(out_weight_hbm, wo.at[0, :, cols(dp, piece)], local_sem.at[6])
        ]
    else:
        out_copies = [
            pltpu.make_async_copy(out_weight_hbm.at[owner], wo.at[at], local_sem.at[6 + at])
            for at, owner in enumerate((me, twin))
        ]
    for copy in locals_ + out_copies:
        copy.start()

    def remote(src, dst, send, recv, device):
        return pltpu.make_async_remote_copy(
            src_ref=src,
            dst_ref=dst,
            send_sem=send,
            recv_sem=recv,
            device_id=device,
            device_id_type=MESH,
        )

    def near(src, dst, send, recv, index):
        return remote(src, dst, send, recv, {"seq": index})

    to_twin = near(tokens_hbm.at[0], tok.at[me], tok_send.at[1], tok_recv.at[1], twin)
    to_partner = near(tokens_hbm.at[0], tok.at[me], tok_send.at[0], tok_recv.at[0], partner)
    forward = near(tok.at[twin], tok.at[twin], tok_send.at[2], tok_recv.at[2], partner)
    cache_copies = []
    for group, owner in enumerate((partner, diag)):
        for at, (hbm, buf) in enumerate(((keys_hbm, kc), (values_hbm, vc))):
            cache_copies.append(
                near(
                    hbm.at[0, :, cols(owner, width)],
                    buf.at[group, core],
                    cache_send.at[2 * group + at],
                    cache_recv.at[2 * group + at],
                    partner,
                )
            )
    if gather:
        weight_twin = near(
            out_weight_hbm, wo.at[1, :, cols(dp, piece)], x_sem.at[0], x_sem.at[1], twin
        )
        z, y = dp // ROW, dp % ROW
        has_up, has_down = z < LINE - 1, z > 0
        above = jnp.minimum(dp + ROW, DP - 1)
        below = jnp.maximum(dp - ROW, 0)
        beside = dp + 1 - 2 * y

        def carry(part, slot, origin, device):
            at = wo.at[part, :, cols(origin, piece)]
            return remote(at, at, w_send.at[part, slot], w_recv.at[part, slot], {"dp": device})

        def up(part, j):
            return carry(part, j, jnp.maximum(dp - ROW * j, 0), above)

        def down(part, j):
            return carry(part, LINE - 1 + j, jnp.minimum(dp + ROW * j, DP - 1), below)

        def across(part, j):
            return carry(part, 2 * LINE - 2 + j, (dp + DP - ROW * j) % DP, beside)

        def step(part, j):
            @pl.when(z >= j)
            def _():
                up(part, j - 1).wait_recv()
                if j < LINE - 1:
                    pl.when(has_up)(lambda: up(part, j).start())
                across(part, j).start()

            @pl.when(z + j < LINE)
            def _():
                down(part, j - 1).wait_recv()
                if j < LINE - 1:
                    pl.when(has_down)(lambda: down(part, j).start())
                across(part, LINE - j).start()

        def begin_down(part):
            pl.when(has_down)(lambda: down(part, 0).start())
            pl.when(y == 1)(lambda: across(part, 0).start())

        def begin_up(part):
            pl.when(has_up)(lambda: up(part, 0).start())
            pl.when(y == 0)(lambda: across(part, 0).start())

    def steps(part, j):
        return (lambda: step(part, j)) if gather else (lambda: None)

    barrier = pltpu.get_barrier_semaphore()

    def tell(sem, index):
        pl.semaphore_signal(sem, inc=1, device_id={"seq": index}, device_id_type=MESH)

    @pl.when(me == 1)
    def _():
        tell(barrier, 0)
        tell(barrier, 3)

    @pl.when(me == 3)
    def _():
        tell(barrier, 2)

    @pl.when(me != 1)
    def _():
        pl.semaphore_wait(barrier, 1 + (me == 2).astype(jnp.int32))

    @pl.when(me == 0)
    def _():
        tell(barrier, 2)
        tell(ready.at[0], 1)

    @pl.when(me == 2)
    def _():
        tell(ready.at[2], 0)
        tell(ready.at[2], 1)
        tell(ready.at[2], 3)

    @pl.when(me == 3)
    def _():
        tell(ready.at[3], 1)

    def cross():
        if gather:
            weight_twin.start()
        to_twin.start()

    @pl.when(chip == 1)
    def _():
        cross()

    @pl.when(me == 1)
    def _():
        pl.semaphore_wait(ready.at[0], 1)

    @pl.when(me == 3)
    def _():
        pl.semaphore_wait(ready.at[2], 1)

    to_partner.start()
    for copy in cache_copies:
        copy.start()

    @pl.when(me == 0)
    def _():
        pl.semaphore_wait(ready.at[2], 1)

    @pl.when(me == 1)
    def _():
        pl.semaphore_wait(ready.at[3], 1)

    @pl.when(chip == 0)
    def _():
        cross()

    @pl.when(me == LEADER)
    def _():
        pl.semaphore_wait(ready.at[2], 1)

    def tell_far(sem, index):
        pl.semaphore_signal(sem, inc=1, device_id={"dp": index}, device_id_type=MESH)

    def spread_word(sem):
        @pl.when(me == LEADER)
        def _():
            for index in (0, 2, 3):
                tell(sem, index)

        @pl.when(me != LEADER)
        def _():
            pl.semaphore_wait(sem, 1)

    if gather:
        @pl.when(me == LEADER)
        def _():
            pl.when(has_up)(lambda: tell_far(barrier, above))
            pl.when(y == 0)(lambda: tell_far(barrier, beside))

            @pl.when(z + y > 0)
            def _():
                pl.semaphore_wait(barrier, has_down.astype(jnp.int32) + y)

            pl.when(has_down)(lambda: tell_far(up_sem.at[0], below))
            pl.when(y == 1)(lambda: tell_far(up_sem.at[1], beside))

        spread_word(far_ready.at[0])
        out_copies[0].wait()
        begin_down(0)

    def far_begin():
        @pl.when(me == LEADER)
        def _():
            pl.when(has_up)(lambda: pl.semaphore_wait(up_sem.at[0], 1))
            pl.when(y == 0)(lambda: pl.semaphore_wait(up_sem.at[1], 1))

        spread_word(far_ready.at[1])
        begin_up(0)
        weight_twin.wait_recv()
        begin_down(1)
        begin_up(1)

    bias = bias_ref[:, cols(me, 3 * width)]
    low = lanes(rows) < HEAD_DIM
    ones = jnp.ones((rows, LANES), BF16)
    none = jnp.zeros((rows, LANES), BF16)

    def markers(count):
        lane = lanes(count)
        return (jnp.where(lane == at, 1.0, 0.0).astype(BF16) for at in (HEAD_DIM, 0))

    middle, first = markers(rows)

    def project(block):
        inputs = tok[block]
        side_, here_ = block // 2, rows_of(block % 2, rows)
        at = rows_of(old // rows + block, rows)
        for pair in range(heads // 2):
            here = slice(6 * pair * HEAD_DIM, 6 * (pair + 1) * HEAD_DIM)
            summed = jnp.dot(inputs, weight[:, here], preferred_element_type=F32) + bias[:, here]
            a, b, c = (summed[:, i * LANES : (i + 1) * LANES] for i in range(3))
            query = (jnp.where(low, a, b).astype(BF16).astype(F32) * HEAD_DIM**-0.5).astype(BF16)
            key = pltpu.roll(jnp.where(low, c, a), HEAD_DIM, 1).astype(BF16)
            value = jnp.where(low, b, c).astype(BF16)
            qo[block, :, pair * LANES : (pair + 1) * LANES] = query
            even, odd = split(query, middle, first)
            q0[side_, 2 * pair, here_], q0[side_, 2 * pair + 1, here_] = even, odd
            k0[2 * pair, at], k0[2 * pair + 1, at] = split(key, none, none)
            v0[2 * pair, at], v0[2 * pair + 1, at] = split(value, ones, ones)

    def query_copy(block):
        return near(qo.at[block], qt.at[block], q_send.at[block], q_recv.at[block], twin)

    def prepare(group, keys, values):
        lane_ = lanes(cache_rows)
        for c in range(2):
            place = lax.broadcasted_iota(jnp.int32, (cache_rows, LANES), 0)
            live = (2 * chip + c) * cache_rows + place < cached
            scale = jnp.where(live, 1.0, 0.0).astype(BF16)
            cap = jnp.where(live, 0.0, DEAD)
            cap_even = jnp.where(lane_ == HEAD_DIM, cap, 0.0).astype(BF16)
            cap_odd = jnp.where(lane_ == 0, cap, 0.0).astype(BF16)
            full = jnp.ones((cache_rows, LANES), BF16)
            at = slice(c * cache_rows, (c + 1) * cache_rows)
            for pair in range(heads // 2):
                here = slice(pair * LANES, (pair + 1) * LANES)
                key = kc[group, c, :, here] * scale
                keys[2 * pair, at], keys[2 * pair + 1, at] = split(key, cap_even, cap_odd)
                value = vc[group, c, :, here]
                values[2 * pair, at], values[2 * pair + 1, at] = split(value, full, full)

    def own_heads(side_, base, between=()):
        tops, products = attend(
            heads,
            lambda h: q0[side_, h],
            [lambda h: k0[h, 0:old], lambda h: k0[h, old : old + new_rows]],
            [lambda h: v0[h, 0:old], lambda h: v0[h, old : old + new_rows]],
            [None, caps[side_]],
            between,
        )
        return finish(tops, products, base)

    def twin_heads(side_, base, between=()):
        marks = list(markers(half))
        queries = []
        both = qt[pl.ds(2 * side_, 2)].reshape(half, width)
        for pair in range(heads // 2):
            queries.extend(split(both[:, pair * LANES : (pair + 1) * LANES], *marks))
        tops, products = attend(
            heads,
            lambda h: queries[h],
            [lambda h: k1[h]],
            [lambda h: v1[h]],
            [None],
            between,
        )
        return finish(tops, products, base)

    def part_copy(group, block):
        return near(
            part_send.at[group, block],
            part_recv.at[1 - group, block],
            p_send.at[group, block],
            p_recv.at[1 - group, block],
            twin,
        )

    stat_copy = near(stat_send, stat_recv, s_sem.at[0], s_sem.at[1], twin)

    locals_[0].wait()
    locals_[1].wait()
    project(me)
    to_partner.wait_recv()
    project(partner)

    for side_ in range(2):
        row = side_ * half + lax.broadcasted_iota(jnp.int32, (half, new_rows), 0)
        new = lax.broadcasted_iota(jnp.int32, (half, new_rows), 1)
        caps[side_] = jnp.where((new <= row) & (new < filled), LIVE, DEAD)
    for at in (0, 1):
        locals_[2 + at].wait()
        cache_copies[at].wait_recv()
    prepare(0, k0, v0)
    query_copy(me).start()
    query_copy(partner).start()
    for at in (2, 3):
        locals_[2 + at].wait()
        cache_copies[at].wait_recv()
    prepare(1, k1, v1)
    if gather:
        far_begin()
        step(0, 1)

    to_twin.wait_recv()
    forward.start()
    project(twin)
    query_copy(twin).start()
    forward.wait_recv()
    project(diag)
    query_copy(diag).start()
    if gather:
        step(1, 1)

    def send_part(group, parts):
        for pair in range(heads // 2):
            both = parts[pair].astype(BF16)
            for block in range(2):
                part_send[group, block, :, pair * LANES : (pair + 1) * LANES] = both[
                    block * rows : (block + 1) * rows
                ]
        for block in (1 - core, core):
            part_copy(group, block).start()

    def keep_part(group, parts):
        for pair in range(heads // 2):
            for block in range(2):
                at = group * width + pair * LANES
                keep[block, :, at : at + LANES] = parts[pair][block * rows : (block + 1) * rows]

    parts, stat = own_heads(1 - chip, heads, [lambda: None, steps(0, 2)])
    send_part(0, parts)
    send_stat[...] = stat
    steps(1, 2)()

    query_copy(twin).wait_recv()
    query_copy(diag).wait_recv()
    parts, stat = twin_heads(1 - chip, 0, [lambda: None, lambda: None, steps(0, 3)])
    send_part(1, parts)
    stat = stat + send_stat[...]
    for block in range(2):
        stat_send[:, block * rows : (block + 1) * rows] = stat[
            block * rows : (block + 1) * rows
        ].T[0 : 2 * heads]
    stat_copy.start()

    parts, stat = own_heads(chip, 0, [steps(1, 3)])
    keep_part(0, parts)
    keep_stat[...] = stat.reshape(2, rows, LANES)
    query_copy(me).wait_recv()
    query_copy(partner).wait_recv()
    parts, stat = twin_heads(chip, heads)
    keep_part(1, parts)
    keep_stat[...] = keep_stat[...] + stat.reshape(2, rows, LANES)

    for copy in out_copies if not gather else []:
        copy.wait()
    if gather:
        for part in range(2):
            for j in range(LINE):
                across(part, j).wait_recv()

    stat_copy.wait_recv()

    def combine(block):
        for group in range(2):
            part_copy(1 - group, block).wait_recv()
        other = jnp.concatenate(
            [
                stat_recv[:, cols(block, rows)],
                jnp.zeros((rows - 2 * heads, rows), F32),
            ],
            0,
        ).T
        share = 1.0 / (1.0 + jnp.exp(other - keep_stat[block]))
        total = 0.0
        for group in range(2):
            at = slice(group * width, (group + 1) * width)
            theirs = part_recv[group, block].astype(F32)
            attn = theirs + spread(share, group * heads, heads) * (keep[block, :, at] - theirs)
            total = total + jnp.dot(attn.astype(BF16), wo[group], preferred_element_type=F32)
        return total

    mixed_copy = near(mixed_send, mixed_recv, m_sem.at[0], m_sem.at[1], partner)
    mixed_send[...] = combine(1 - core).astype(BF16)
    mixed_copy.start()
    mixed = combine(core) + out_bias_ref[...] + tok[me].astype(F32)
    mixed_copy.wait_recv()
    mixed = mixed + mixed_recv[...].astype(F32)
    center = mixed - jnp.mean(mixed, axis=1, keepdims=True)
    variance = jnp.mean(center * center, axis=1, keepdims=True)
    normed = center * lax.rsqrt(variance + 1e-05) * gain_ref[...] + shift_ref[...]
    out_ref[0] = normed.astype(BF16)

    sent = [to_partner, forward, stat_copy, mixed_copy] + cache_copies
    sent += [to_twin] + [query_copy(b) for b in range(tok.shape[0])]
    sent += [part_copy(g, b) for g in range(2) for b in range(2)]
    if gather:
        sent.append(weight_twin)
        for part in range(2):
            sent += [across(part, j) for j in range(LINE)]
            for j in range(LINE - 1):
                pl.when(has_up & (z >= j))(up(part, j).wait_send)
                pl.when(has_down & (z + j < LINE))(down(part, j).wait_send)
    for copy in sent:
        copy.wait_send()


def local(
    tokens,
    cache_keys,
    cache_values,
    qkv_weight,
    qkv_bias,
    out_weight,
    out_bias,
    norm_gain,
    norm_bias,
    cached_len,
    span_len,
    slot_request,
):
    rows, model = tokens.shape[1:]
    cache_rows = cache_keys.shape[1]
    width = qkv_weight.shape[1] // 3
    heads = width // HEAD_DIM
    blocks = lax.axis_size("seq")
    half = 2 * rows
    old = 2 * cache_rows
    total = old + blocks * rows
    hbm = pl.BlockSpec(memory_space=pltpu.HBM)
    vmem = pl.BlockSpec(memory_space=pltpu.VMEM)
    smem = pl.BlockSpec(memory_space=pltpu.SMEM)
    dma = pltpu.SemaphoreType.DMA

    gather = lax.axis_size("dp") == DP and out_weight.shape[1] % 128 == 0
    if not gather:
        out_weight = lax.all_gather(out_weight, "dp", axis=1, tiled=True)
        out_weight = lax.all_gather(out_weight, "seq", axis=0)

    return pl.pallas_call(
        functools.partial(kernel, gather),
        out_shape=jax.ShapeDtypeStruct((1, rows, model), BF16),
        in_specs=[smem] * 3 + [hbm] * 5 + [vmem] * 4,
        out_specs=vmem,
        scratch_shapes=[
            pltpu.VMEM((blocks, rows, model), BF16),
            pltpu.VMEM((model, 3 * width), BF16),
            pltpu.VMEM((2, 2, cache_rows, width), BF16),
            pltpu.VMEM((2, 2, cache_rows, width), BF16),
            pltpu.VMEM((heads, total, LANES), BF16),
            pltpu.VMEM((heads, total, LANES), BF16),
            pltpu.VMEM((heads, old, LANES), BF16),
            pltpu.VMEM((heads, old, LANES), BF16),
            pltpu.VMEM((2, heads, half, LANES), BF16),
            pltpu.VMEM((blocks, rows, width), BF16),
            pltpu.VMEM((blocks, rows, width), BF16),
            pltpu.VMEM((2, half, blocks * rows), F32),
            pltpu.VMEM((2, rows, 2 * width), F32),
            pltpu.VMEM((2, rows, LANES), F32),
            pltpu.VMEM((half, LANES), F32),
            pltpu.VMEM((2, 2, rows, width), BF16),
            pltpu.VMEM((2, 2, rows, width), BF16),
            pltpu.VMEM((2 * heads, half), F32),
            pltpu.VMEM((2 * heads, half), F32),
            pltpu.VMEM((rows, model), BF16),
            pltpu.VMEM((rows, model), BF16),
            pltpu.VMEM((2, width, model), BF16),
            dma((8,)),
            dma((3,)),
            dma((3,)),
            dma((4,)),
            dma((4,)),
            dma((blocks,)),
            dma((blocks,)),
            dma((2, 2)),
            dma((2, 2)),
            dma((2,)),
            dma((2,)),
            dma((2,)),
            dma((2, 3 * LINE - 2)),
            dma((2, 3 * LINE - 2)),
            pltpu.SemaphoreType.REGULAR((4,)),
            pltpu.SemaphoreType.REGULAR((2,)),
            pltpu.SemaphoreType.REGULAR((2,)),
        ],
        compiler_params=pltpu.CompilerParams(
            collective_id=0, has_side_effects=True, vmem_limit_bytes=60 << 20
        ),
        cost_estimate=pl.CostEstimate(
            flops=6_000_000_000, bytes_accessed=6_000_000, transcendentals=5_000_000
        ),
        name="sublayer",
    )(
        cached_len,
        span_len,
        slot_request,
        tokens,
        cache_keys,
        cache_values,
        qkv_weight,
        out_weight,
        qkv_bias.reshape(1, -1),
        out_bias.reshape(1, -1),
        norm_gain.reshape(1, -1),
        norm_bias.reshape(1, -1),
    )


def solution(mesh):
    return jax.shard_map(
        local,
        mesh=mesh,
        in_specs=(
            P("dp", "seq", None),
            P("dp", "seq", None),
            P("dp", "seq", None),
            P(None, "seq"),
            P(),
            P("seq", "dp"),
            P(),
            P(),
            P(),
            P(),
            P(),
            P(),
        ),
        out_specs=P("dp", "seq", None),
        check_vma=False,
    )
```

```python
import functools

import jax
import jax.numpy as jnp
from jax import lax
from jax.experimental import pallas as pl
from jax.experimental.pallas import tpu as pltpu
from jax.sharding import PartitionSpec as P

HEAD_DIM = 64
LANES = 128
LIVE = 3e38
DEAD = -1e30
F32 = jnp.float32
BF16 = jnp.bfloat16
MESH = pl.DeviceIdType.MESH
LEADER = 1
DP = 8
ROW = 2
LINE = DP // ROW


def nothing():
    pass


def peers():
    me = lax.axis_index("seq")
    core = me % 2
    partner = me + 1 - 2 * core
    twin = (me + 2) % 4
    diag = (partner + 2) % 4
    return me, core, partner, twin, diag


def cols(index, width):
    return pl.ds(pl.multiple_of(index * width, 128), width)


def rows_of(index, height):
    return pl.ds(pl.multiple_of(index * height, 128), height)


def nt(a, b):
    return lax.dot_general(a, b, (((1,), (1,)), ((), ())), preferred_element_type=F32)


def lanes(rows):
    return lax.broadcasted_iota(jnp.int32, (rows, LANES), 1)


def split(pair, even, odd):
    low = lanes(pair.shape[0]) < HEAD_DIM
    return jnp.where(low, pair, even), jnp.where(low, odd, pair)


def attend(heads, query, keys, values, caps, between=()):
    def scores(h):
        out = []
        for k, cap in zip(keys, caps):
            s = nt(query(h), k(h))
            out.append(s if cap is None else jnp.minimum(s, cap))
        return out

    now = scores(0)
    tops, products = [], []
    for h in range(heads):
        later = scores(h + 1) if h + 1 < heads else None
        top = functools.reduce(jnp.maximum, [jnp.max(s, 1, keepdims=True) for s in now])
        product = 0.0
        for s, v in zip(now, values):
            product = product + jnp.dot(
                jnp.exp(s - top).astype(BF16), v(h), preferred_element_type=F32
            )
        tops.append(top)
        products.append(product)
        now = later
        if h < len(between):
            between[h]()
    return tops, products


def finish(tops, products):
    rows = products[0].shape[0]
    lane = lanes(rows)
    low = lane < HEAD_DIM
    parts = []
    left = jnp.zeros((rows, LANES), F32)
    right = jnp.zeros((rows, LANES), F32)
    for pair in range(len(products) // 2):
        a, b = products[2 * pair], products[2 * pair + 1]
        total = jnp.where(low, b, a)
        log = jnp.log(total)
        right = jnp.where(lane == HEAD_DIM + 2 * pair, tops[2 * pair] + log, right)
        left = jnp.where(lane == 2 * pair + 1, tops[2 * pair + 1] + log, left)
        parts.append(jnp.where(low, a, b) / pltpu.roll(total, HEAD_DIM, 1))
    return parts, left + pltpu.roll(right, HEAD_DIM, 1)


def spread(tile, heads):
    low = lanes(tile.shape[0]) < HEAD_DIM
    out = []
    for at in range(0, heads, 2):
        out.append(jnp.where(low, tile[:, at : at + 1], tile[:, at + 1 : at + 2]))
    return jnp.concatenate(out, 1)


def kernel(
    gather,
    cached_ref,
    span_ref,
    slot_ref,
    tokens_hbm,
    keys_hbm,
    values_hbm,
    weight_hbm,
    out_weight_hbm,
    bias_ref,
    out_bias_ref,
    gain_ref,
    shift_ref,
    out_ref,
    tok,
    weight,
    kc,
    vc,
    k0,
    v0,
    k1,
    v1,
    q0,
    qo,
    qt,
    near_cap,
    caps,
    own_top,
    own_product,
    keep,
    keep_stat,
    mixed_sum,
    part_send,
    part_recv,
    stat_send,
    stat_recv,
    mixed_send,
    mixed_recv,
    wo,
    local_sem,
    tok_send,
    tok_recv,
    cache_send,
    cache_recv,
    q_send,
    q_recv,
    p_send,
    p_recv,
    s_sem,
    m_sem,
    x_sem,
    w_send,
    w_recv,
    ready,
    up_sem,
    far_ready,
):
    me, core, partner, twin, diag = peers()
    chip = me // 2
    rows = tok.shape[1]
    half = 2 * rows
    cache_rows = kc.shape[2]
    old = 2 * cache_rows
    width = kc.shape[3]
    heads = width // HEAD_DIM
    dp = lax.axis_index("dp")
    request = slot_ref[dp]
    cached = cached_ref[request]
    filled = span_ref[request]
    new_rows = tok.shape[0] * rows

    locals_ = [
        pltpu.make_async_copy(tokens_hbm.at[0], tok.at[me], local_sem.at[0]),
        pltpu.make_async_copy(weight_hbm, weight, local_sem.at[1]),
    ]
    for group, owner in enumerate((me, twin)):
        for at, (hbm, buf) in enumerate(((keys_hbm, kc), (values_hbm, vc))):
            locals_.append(
                pltpu.make_async_copy(
                    hbm.at[0, :, cols(owner, width)],
                    buf.at[group, core],
                    local_sem.at[2 + 2 * group + at],
                )
            )
    if gather:
        piece = out_weight_hbm.shape[1]
        out_copies = [
            pltpu.make_async_copy(out_weight_hbm, wo.at[0, :, cols(dp, piece)], local_sem.at[6])
        ]
    else:
        out_copies = [
            pltpu.make_async_copy(out_weight_hbm.at[owner], wo.at[at], local_sem.at[6 + at])
            for at, owner in enumerate((me, twin))
        ]
    for copy in locals_ + out_copies:
        copy.start()

    def remote(src, dst, send, recv, device):
        return pltpu.make_async_remote_copy(
            src_ref=src,
            dst_ref=dst,
            send_sem=send,
            recv_sem=recv,
            device_id=device,
            device_id_type=MESH,
        )

    def near(src, dst, send, recv, index):
        return remote(src, dst, send, recv, {"seq": index})

    to_twin = near(tokens_hbm.at[0], tok.at[me], tok_send.at[1], tok_recv.at[1], twin)
    to_partner = near(tokens_hbm.at[0], tok.at[me], tok_send.at[0], tok_recv.at[0], partner)
    forward = near(tok.at[twin], tok.at[twin], tok_send.at[2], tok_recv.at[2], partner)
    cache_copies = []
    for group, owner in enumerate((partner, diag)):
        for at, (hbm, buf) in enumerate(((keys_hbm, kc), (values_hbm, vc))):
            cache_copies.append(
                near(
                    hbm.at[0, :, cols(owner, width)],
                    buf.at[group, core],
                    cache_send.at[2 * group + at],
                    cache_recv.at[2 * group + at],
                    partner,
                )
            )
    if gather:
        weight_twin = near(
            out_weight_hbm, wo.at[1, :, cols(dp, piece)], x_sem.at[0], x_sem.at[1], twin
        )
        z, y = dp // ROW, dp % ROW
        has_up, has_down = z < LINE - 1, z > 0
        above = jnp.minimum(dp + ROW, DP - 1)
        below = jnp.maximum(dp - ROW, 0)
        beside = dp + 1 - 2 * y

        def carry(part, slot, origin, device):
            at = wo.at[part, :, cols(origin, piece)]
            return remote(at, at, w_send.at[part, slot], w_recv.at[part, slot], {"dp": device})

        def up(part, j):
            return carry(part, j, jnp.maximum(dp - ROW * j, 0), above)

        def down(part, j):
            return carry(part, LINE - 1 + j, jnp.minimum(dp + ROW * j, DP - 1), below)

        def across(part, j):
            return carry(part, 2 * LINE - 2 + j, (dp + DP - ROW * j) % DP, beside)

        def step(part, j):
            @pl.when(z >= j)
            def _():
                up(part, j - 1).wait_recv()
                if j < LINE - 1:
                    pl.when(has_up)(lambda: up(part, j).start())
                across(part, j).start()

            @pl.when(z + j < LINE)
            def _():
                down(part, j - 1).wait_recv()
                if j < LINE - 1:
                    pl.when(has_down)(lambda: down(part, j).start())
                across(part, LINE - j).start()

        def begin_down(part):
            pl.when(has_down)(lambda: down(part, 0).start())
            pl.when(y == 1)(lambda: across(part, 0).start())

        def begin_up(part):
            pl.when(has_up)(lambda: up(part, 0).start())
            pl.when(y == 0)(lambda: across(part, 0).start())

    def steps(part, j):
        return (lambda: step(part, j)) if gather else nothing

    barrier = pltpu.get_barrier_semaphore()

    def tell(sem, index):
        pl.semaphore_signal(sem, inc=1, device_id={"seq": index}, device_id_type=MESH)

    @pl.when(me == 1)
    def _():
        tell(barrier, 0)
        tell(barrier, 3)

    @pl.when(me == 3)
    def _():
        tell(barrier, 2)

    @pl.when(me != 1)
    def _():
        pl.semaphore_wait(barrier, 1 + (me == 2).astype(jnp.int32))

    @pl.when(me == 0)
    def _():
        tell(barrier, 2)
        tell(ready.at[0], 1)

    @pl.when(me == 2)
    def _():
        tell(ready.at[2], 0)
        tell(ready.at[2], 1)
        tell(ready.at[2], 3)

    @pl.when(me == 3)
    def _():
        tell(ready.at[3], 1)

    def cross():
        if gather:
            weight_twin.start()
        to_twin.start()

    @pl.when(chip == 1)
    def _():
        cross()

    @pl.when(me == 1)
    def _():
        pl.semaphore_wait(ready.at[0], 1)

    @pl.when(me == 3)
    def _():
        pl.semaphore_wait(ready.at[2], 1)

    to_partner.start()
    for copy in cache_copies:
        copy.start()

    @pl.when(me == 0)
    def _():
        pl.semaphore_wait(ready.at[2], 1)

    @pl.when(me == 1)
    def _():
        pl.semaphore_wait(ready.at[3], 1)

    @pl.when(chip == 0)
    def _():
        cross()

    @pl.when(me == LEADER)
    def _():
        pl.semaphore_wait(ready.at[2], 1)

    def tell_far(sem, index):
        pl.semaphore_signal(sem, inc=1, device_id={"dp": index}, device_id_type=MESH)

    def spread_word(sem):
        @pl.when(me == LEADER)
        def _():
            for index in (0, 2, 3):
                tell(sem, index)

        @pl.when(me != LEADER)
        def _():
            pl.semaphore_wait(sem, 1)

    if gather:
        @pl.when(me == LEADER)
        def _():
            pl.when(has_up)(lambda: tell_far(barrier, above))
            pl.when(y == 0)(lambda: tell_far(barrier, beside))

            @pl.when(z + y > 0)
            def _():
                pl.semaphore_wait(barrier, has_down.astype(jnp.int32) + y)

            pl.when(has_down)(lambda: tell_far(up_sem.at[0], below))
            pl.when(y == 1)(lambda: tell_far(up_sem.at[1], beside))

        spread_word(far_ready.at[0])
        out_copies[0].wait()
        begin_down(0)

    def far_begin():
        @pl.when(me == LEADER)
        def _():
            pl.when(has_up)(lambda: pl.semaphore_wait(up_sem.at[0], 1))
            pl.when(y == 0)(lambda: pl.semaphore_wait(up_sem.at[1], 1))

        spread_word(far_ready.at[1])
        begin_up(0)

        @pl.when(z < LINE // 2)
        def _():
            weight_twin.wait_recv()
            begin_down(1)

        begin_up(1)

    def far_early():
        @pl.when(z >= LINE // 2)
        def _():
            weight_twin.wait_recv()
            begin_down(1)

    bias = bias_ref[:, cols(me, 3 * width)]
    low = lanes(rows) < HEAD_DIM
    ones = jnp.ones((rows, LANES), BF16)
    none = jnp.zeros((rows, LANES), BF16)

    def markers(count):
        lane = lanes(count)
        return (jnp.where(lane == at, 1.0, 0.0).astype(BF16) for at in (HEAD_DIM, 0))

    middle, first = markers(rows)

    def project(block):
        inputs = tok[block]
        side_, here_ = block // 2, rows_of(block % 2, rows)
        at = rows_of(old // rows + block, rows)
        for pair in range(heads // 2):
            here = slice(6 * pair * HEAD_DIM, 6 * (pair + 1) * HEAD_DIM)
            summed = jnp.dot(inputs, weight[:, here], preferred_element_type=F32) + bias[:, here]
            a, b, c = (summed[:, i * LANES : (i + 1) * LANES] for i in range(3))
            query = (jnp.where(low, a, b).astype(BF16).astype(F32) * HEAD_DIM**-0.5).astype(BF16)
            key = pltpu.roll(jnp.where(low, c, a), HEAD_DIM, 1).astype(BF16)
            value = jnp.where(low, b, c).astype(BF16)
            qo[block, :, pair * LANES : (pair + 1) * LANES] = query
            even, odd = split(query, middle, first)
            q0[side_, 2 * pair, here_], q0[side_, 2 * pair + 1, here_] = even, odd
            k0[2 * pair, at], k0[2 * pair + 1, at] = split(key, none, none)
            v0[2 * pair, at], v0[2 * pair + 1, at] = split(value, ones, ones)

    def query_copy(block):
        return near(qo.at[block], qt.at[block], q_send.at[block], q_recv.at[block], twin)

    def prepare(group, keys, values):
        lane_ = lanes(cache_rows)
        for c in range(2):
            place = lax.broadcasted_iota(jnp.int32, (cache_rows, LANES), 0)
            live = (2 * chip + c) * cache_rows + place < cached
            scale = jnp.where(live, 1.0, 0.0).astype(BF16)
            cap = jnp.where(live, 0.0, DEAD)
            cap_even = jnp.where(lane_ == HEAD_DIM, cap, 0.0).astype(BF16)
            cap_odd = jnp.where(lane_ == 0, cap, 0.0).astype(BF16)
            full = jnp.ones((cache_rows, LANES), BF16)
            at = slice(c * cache_rows, (c + 1) * cache_rows)
            for pair in range(heads // 2):
                here = slice(pair * LANES, (pair + 1) * LANES)
                key = kc[group, c, :, here] * scale
                keys[2 * pair, at], keys[2 * pair + 1, at] = split(key, cap_even, cap_odd)
                value = vc[group, c, :, here]
                values[2 * pair, at], values[2 * pair + 1, at] = split(value, full, full)

    def cached_keys(keys, values):
        return (lambda h: keys[h, 0:old]), (lambda h: values[h, 0:old])

    def new_keys(start, count):
        at = rows_of(old // half + start, half) if count == half else pl.ds(old, count)
        return (lambda h: k0[h, at]), (lambda h: v0[h, at])

    def own_heads(side_, fresh, cap, between=()):
        parts = [cached_keys(k0, v0), fresh]
        return attend(
            heads,
            lambda h: q0[side_, h],
            [k for k, _ in parts],
            [v for _, v in parts],
            [None, cap],
            between,
        )

    def twin_heads(side_, between=()):
        marks = list(markers(half))
        queries = []
        both = qt[pl.ds(2 * side_, 2)].reshape(half, width)
        for pair in range(heads // 2):
            queries.extend(split(both[:, pair * LANES : (pair + 1) * LANES], *marks))
        k, v = cached_keys(k1, v1)
        return attend(heads, lambda h: queries[h], [k], [v], [None], between)

    def part_copy(group, block):
        return near(
            part_send.at[group, block],
            part_recv.at[1 - group, block],
            p_send.at[group, block],
            p_recv.at[1 - group, block],
            twin,
        )

    def stat_copy(group):
        return near(
            stat_send.at[group],
            stat_recv.at[1 - group],
            s_sem.at[0, group],
            s_sem.at[1, 1 - group],
            twin,
        )

    locals_[0].wait()
    locals_[1].wait()
    project(me)
    to_partner.wait_recv()
    project(partner)

    row = lax.broadcasted_iota(jnp.int32, (half, half), 0)
    new = lax.broadcasted_iota(jnp.int32, (half, half), 1)
    near_cap[...] = jnp.where((new <= row) & (chip * half + new < filled), LIVE, DEAD)
    row = (1 - chip) * half + lax.broadcasted_iota(jnp.int32, (half, new_rows), 0)
    new = lax.broadcasted_iota(jnp.int32, (half, new_rows), 1)
    caps[...] = jnp.where((new <= row) & (new < filled), LIVE, DEAD)
    for at in (0, 1):
        locals_[2 + at].wait()
        cache_copies[at].wait_recv()
    prepare(0, k0, v0)
    query_copy(me).start()
    query_copy(partner).start()
    if gather:
        far_early()
    tops, products = own_heads(
        chip, new_keys(chip, half), near_cap[...], [nothing, far_begin if gather else nothing]
    )
    for h in range(heads):
        own_top[h] = jnp.broadcast_to(tops[h], (half, LANES))
        own_product[h] = products[h]
    for at in (2, 3):
        locals_[2 + at].wait()
        cache_copies[at].wait_recv()
    prepare(1, k1, v1)
    steps(0, 1)()

    to_twin.wait_recv()
    forward.start()
    project(twin)
    query_copy(twin).start()
    forward.wait_recv()
    project(diag)
    query_copy(diag).start()
    steps(1, 1)()

    def send_part(group, tops, products):
        parts, stat = finish(tops, products)
        for pair in range(heads // 2):
            both = parts[pair].astype(BF16)
            for block in range(2):
                part_send[group, block, :, pair * LANES : (pair + 1) * LANES] = both[
                    block * rows : (block + 1) * rows
                ]
        for block in range(2):
            stat_send[group, :, block * rows : (block + 1) * rows] = stat[
                block * rows : (block + 1) * rows
            ].T[0:8]
        for block in (1 - core, core):
            part_copy(group, block).start()
        stat_copy(group).start()

    def keep_part(group, tops, products):
        parts, stat = finish(tops, products)
        for pair in range(heads // 2):
            at = group * width + pair * LANES
            keep[:, :, at : at + LANES] = parts[pair].reshape(2, rows, LANES)
        keep_stat[group] = stat.reshape(2, rows, LANES)

    query_copy(twin).wait_recv()
    query_copy(diag).wait_recv()
    send_part(1, *twin_heads(1 - chip, [nothing, steps(0, 2)]))
    send_part(
        0, *own_heads(1 - chip, new_keys(0, new_rows), caps[...], [steps(1, 2), nothing, steps(0, 3)])
    )

    @pl.when(chip == 1)
    def _():
        fresh = lax.broadcasted_iota(jnp.int32, (1, half), 1) < filled
        k, v = new_keys(0, half)
        tops, products = attend(
            heads, lambda h: q0[1, h], [k], [v], [jnp.where(fresh, LIVE, DEAD)]
        )
        for h in range(heads):
            before = own_top[h]
            top = jnp.maximum(before, tops[h])
            own_product[h] = own_product[h] * jnp.exp(before - top) + products[h] * jnp.exp(
                tops[h] - top
            )
            own_top[h] = top

    keep_part(0, [own_top[h] for h in range(heads)], [own_product[h] for h in range(heads)])
    query_copy(me).wait_recv()
    query_copy(partner).wait_recv()
    keep_part(1, *twin_heads(chip, [nothing, steps(1, 3)]))

    for copy in out_copies if not gather else []:
        copy.wait()
    def weights_there(part):
        if gather:
            for j in range(LINE):
                across(part, j).wait_recv()

    def combine(group, block):
        other = jnp.concatenate(
            [stat_recv[group, :, cols(block, rows)], jnp.zeros((rows - 8, rows), F32)], 0
        ).T
        share = 1.0 / (1.0 + jnp.exp(other - keep_stat[group, block]))
        theirs = part_recv[group, block].astype(F32)
        own = keep[block, :, group * width : (group + 1) * width]
        attn = theirs + spread(share, heads) * (own - theirs)
        return jnp.dot(attn.astype(BF16), wo[group], preferred_element_type=F32)

    mixed_copy = near(mixed_send, mixed_recv, m_sem.at[0], m_sem.at[1], partner)
    weights_there(0)
    stat_copy(1).wait_recv()
    for block in range(2):
        part_copy(1, block).wait_recv()
        mixed_sum[block] = combine(0, block)
    mixed_sum[core] = mixed_sum[core] + out_bias_ref[...] + tok[me].astype(F32)
    weights_there(1)
    stat_copy(0).wait_recv()
    part_copy(0, 1 - core).wait_recv()
    mixed_send[...] = (mixed_sum[1 - core] + combine(1, 1 - core)).astype(BF16)
    mixed_copy.start()
    part_copy(0, core).wait_recv()
    mixed = mixed_sum[core] + combine(1, core)
    mixed_copy.wait_recv()
    mixed = mixed + mixed_recv[...].astype(F32)
    center = mixed - jnp.mean(mixed, axis=1, keepdims=True)
    variance = jnp.mean(center * center, axis=1, keepdims=True)
    normed = center * lax.rsqrt(variance + 1e-05) * gain_ref[...] + shift_ref[...]
    out_ref[0] = normed.astype(BF16)

    sent = [to_partner, forward, stat_copy(0), stat_copy(1), mixed_copy] + cache_copies
    sent += [to_twin] + [query_copy(b) for b in range(tok.shape[0])]
    sent += [part_copy(g, b) for g in range(2) for b in range(2)]
    if gather:
        sent.append(weight_twin)
        for part in range(2):
            sent += [across(part, j) for j in range(LINE)]
            for j in range(LINE - 1):
                pl.when(has_up & (z >= j))(up(part, j).wait_send)
                pl.when(has_down & (z + j < LINE))(down(part, j).wait_send)
    for copy in sent:
        copy.wait_send()


def local(
    tokens,
    cache_keys,
    cache_values,
    qkv_weight,
    qkv_bias,
    out_weight,
    out_bias,
    norm_gain,
    norm_bias,
    cached_len,
    span_len,
    slot_request,
):
    rows, model = tokens.shape[1:]
    cache_rows = cache_keys.shape[1]
    width = qkv_weight.shape[1] // 3
    heads = width // HEAD_DIM
    blocks = lax.axis_size("seq")
    half = 2 * rows
    old = 2 * cache_rows
    total = old + blocks * rows
    hbm = pl.BlockSpec(memory_space=pltpu.HBM)
    vmem = pl.BlockSpec(memory_space=pltpu.VMEM)
    smem = pl.BlockSpec(memory_space=pltpu.SMEM)
    dma = pltpu.SemaphoreType.DMA

    gather = lax.axis_size("dp") == DP and out_weight.shape[1] % 128 == 0
    if not gather:
        out_weight = lax.all_gather(out_weight, "dp", axis=1, tiled=True)
        out_weight = lax.all_gather(out_weight, "seq", axis=0)

    return pl.pallas_call(
        functools.partial(kernel, gather),
        out_shape=pltpu.VMEM((1, rows, model), BF16),
        in_specs=[smem] * 3 + [hbm] * 5 + [vmem] * 4,
        out_specs=vmem,
        scratch_shapes=[
            pltpu.VMEM((blocks, rows, model), BF16),
            pltpu.VMEM((model, 3 * width), BF16),
            pltpu.VMEM((2, 2, cache_rows, width), BF16),
            pltpu.VMEM((2, 2, cache_rows, width), BF16),
            pltpu.VMEM((heads, total, LANES), BF16),
            pltpu.VMEM((heads, total, LANES), BF16),
            pltpu.VMEM((heads, old, LANES), BF16),
            pltpu.VMEM((heads, old, LANES), BF16),
            pltpu.VMEM((2, heads, half, LANES), BF16),
            pltpu.VMEM((blocks, rows, width), BF16),
            pltpu.VMEM((blocks, rows, width), BF16),
            pltpu.VMEM((half, half), F32),
            pltpu.VMEM((half, blocks * rows), F32),
            pltpu.VMEM((heads, half, LANES), F32),
            pltpu.VMEM((heads, half, LANES), F32),
            pltpu.VMEM((2, rows, 2 * width), F32),
            pltpu.VMEM((2, 2, rows, LANES), F32),
            pltpu.VMEM((2, rows, model), F32),
            pltpu.VMEM((2, 2, rows, width), BF16),
            pltpu.VMEM((2, 2, rows, width), BF16),
            pltpu.VMEM((2, 8, half), F32),
            pltpu.VMEM((2, 8, half), F32),
            pltpu.VMEM((rows, model), BF16),
            pltpu.VMEM((rows, model), BF16),
            pltpu.VMEM((2, width, model), BF16),
            dma((8,)),
            dma((3,)),
            dma((3,)),
            dma((4,)),
            dma((4,)),
            dma((blocks,)),
            dma((blocks,)),
            dma((2, 2)),
            dma((2, 2)),
            dma((2, 2)),
            dma((2,)),
            dma((2,)),
            dma((2, 3 * LINE - 2)),
            dma((2, 3 * LINE - 2)),
            pltpu.SemaphoreType.REGULAR((4,)),
            pltpu.SemaphoreType.REGULAR((2,)),
            pltpu.SemaphoreType.REGULAR((2,)),
        ],
        compiler_params=pltpu.CompilerParams(
            collective_id=0, has_side_effects=True, vmem_limit_bytes=60 << 20
        ),
        cost_estimate=pl.CostEstimate(
            flops=6_000_000_000, bytes_accessed=6_000_000, transcendentals=5_000_000
        ),
        name="sublayer",
    )(
        cached_len,
        span_len,
        slot_request,
        tokens,
        cache_keys,
        cache_values,
        qkv_weight,
        out_weight,
        qkv_bias.reshape(1, -1),
        out_bias.reshape(1, -1),
        norm_gain.reshape(1, -1),
        norm_bias.reshape(1, -1),
    )


def solution(mesh):
    return jax.shard_map(
        local,
        mesh=mesh,
        in_specs=(
            P("dp", "seq", None),
            P("dp", "seq", None),
            P("dp", "seq", None),
            P(None, "seq"),
            P(),
            P("seq", "dp"),
            P(),
            P(),
            P(),
            P(),
            P(),
            P(),
        ),
        out_specs=P("dp", "seq", None),
        check_vma=False,
    )
```

```python
import functools

import jax
import jax.numpy as jnp
from jax import lax
from jax.experimental import pallas as pl
from jax.experimental.pallas import tpu as pltpu
from jax.sharding import PartitionSpec as P

HEAD_DIM = 64
LANES = 128
LIVE = 3e38
DEAD = -1e30
F32 = jnp.float32
BF16 = jnp.bfloat16
MESH = pl.DeviceIdType.MESH
LEADER = 1
DP = 8
ROW = 2
LINE = DP // ROW
UP, DOWN = 1, 2


def nothing():
    pass


def peers():
    me = lax.axis_index("seq")
    core = me % 2
    partner = me + 1 - 2 * core
    twin = (me + 2) % 4
    diag = (partner + 2) % 4
    return me, core, partner, twin, diag


def cols(index, width):
    return pl.ds(pl.multiple_of(index * width, 128), width)


def rows_of(index, height):
    return pl.ds(pl.multiple_of(index * height, 128), height)


def nt(a, b):
    return lax.dot_general(a, b, (((1,), (1,)), ((), ())), preferred_element_type=F32)


def lanes(rows):
    return lax.broadcasted_iota(jnp.int32, (rows, LANES), 1)


def split(pair, even, odd):
    low = lanes(pair.shape[0]) < HEAD_DIM
    return jnp.where(low, pair, even), jnp.where(low, odd, pair)


def attend(heads, query, keys, values, caps, between=()):
    def scores(h):
        out = []
        for k, cap in zip(keys, caps):
            s = nt(query(h), k(h))
            out.append(s if cap is None else jnp.minimum(s, cap))
        return out

    now = scores(0)
    tops, products = [], []
    for h in range(heads):
        later = scores(h + 1) if h + 1 < heads else None
        top = functools.reduce(jnp.maximum, [jnp.max(s, 1, keepdims=True) for s in now])
        product = 0.0
        for s, v in zip(now, values):
            product = product + jnp.dot(
                jnp.exp(s - top).astype(BF16), v(h), preferred_element_type=F32
            )
        tops.append(top)
        products.append(product)
        now = later
        if h < len(between):
            between[h]()
    return tops, products


def finish(tops, products):
    rows = products[0].shape[0]
    lane = lanes(rows)
    low = lane < HEAD_DIM
    parts = []
    left = jnp.zeros((rows, LANES), F32)
    right = jnp.zeros((rows, LANES), F32)
    for pair in range(len(products) // 2):
        a, b = products[2 * pair], products[2 * pair + 1]
        total = jnp.where(low, b, a)
        log = jnp.log(total)
        right = jnp.where(lane == HEAD_DIM + 2 * pair, tops[2 * pair] + log, right)
        left = jnp.where(lane == 2 * pair + 1, tops[2 * pair + 1] + log, left)
        parts.append(jnp.where(low, a, b) / pltpu.roll(total, HEAD_DIM, 1))
    return parts, left + pltpu.roll(right, HEAD_DIM, 1)


def spread(tile, heads):
    low = lanes(tile.shape[0]) < HEAD_DIM
    out = []
    for at in range(0, heads, 2):
        out.append(jnp.where(low, tile[:, at : at + 1], tile[:, at + 1 : at + 2]))
    return jnp.concatenate(out, 1)


def kernel(
    gather,
    cached_ref,
    span_ref,
    slot_ref,
    tokens_hbm,
    keys_hbm,
    values_hbm,
    weight_hbm,
    out_weight_hbm,
    bias_ref,
    out_bias_ref,
    gain_ref,
    shift_ref,
    out_ref,
    tok,
    weight,
    kc,
    vc,
    k0,
    v0,
    k1,
    v1,
    q0,
    qo,
    qt,
    near_cap,
    caps,
    own_top,
    own_product,
    keep,
    keep_stat,
    rest,
    mixed_sum,
    part_send,
    part_recv,
    stat_send,
    stat_recv,
    mixed_send,
    mixed_recv,
    wo,
    local_sem,
    tok_send,
    tok_recv,
    cache_send,
    cache_recv,
    q_send,
    q_recv,
    p_send,
    p_recv,
    s_sem,
    m_sem,
    x_sem,
    w_send,
    w_recv,
    ready,
    up_sem,
    far_ready,
):
    me, core, partner, twin, diag = peers()
    chip = me // 2
    rows = tok.shape[1]
    half = 2 * rows
    cache_rows = kc.shape[2]
    old = 2 * cache_rows
    width = kc.shape[3]
    heads = width // HEAD_DIM
    dp = lax.axis_index("dp")
    request = slot_ref[dp]
    cached = cached_ref[request]
    filled = span_ref[request]
    new_rows = tok.shape[0] * rows

    locals_ = [
        pltpu.make_async_copy(tokens_hbm.at[0], tok.at[me], local_sem.at[0]),
        pltpu.make_async_copy(weight_hbm, weight, local_sem.at[1]),
    ]
    for group, owner in enumerate((me, twin)):
        for at, (hbm, buf) in enumerate(((keys_hbm, kc), (values_hbm, vc))):
            locals_.append(
                pltpu.make_async_copy(
                    hbm.at[0, :, cols(owner, width)],
                    buf.at[group, core],
                    local_sem.at[2 + 2 * group + at],
                )
            )
    if gather:
        piece = out_weight_hbm.shape[1]
        out_copies = [
            pltpu.make_async_copy(out_weight_hbm, wo.at[0, :, cols(dp, piece)], local_sem.at[6])
        ]
    else:
        out_copies = [
            pltpu.make_async_copy(out_weight_hbm.at[owner], wo.at[at], local_sem.at[6 + at])
            for at, owner in enumerate((me, twin))
        ]
    for copy in locals_ + out_copies:
        copy.start()

    def remote(src, dst, send, recv, device):
        return pltpu.make_async_remote_copy(
            src_ref=src,
            dst_ref=dst,
            send_sem=send,
            recv_sem=recv,
            device_id=device,
            device_id_type=MESH,
        )

    def near(src, dst, send, recv, index):
        return remote(src, dst, send, recv, {"seq": index})

    to_twin = near(tokens_hbm.at[0], tok.at[me], tok_send.at[1], tok_recv.at[1], twin)
    to_partner = near(tokens_hbm.at[0], tok.at[me], tok_send.at[0], tok_recv.at[0], partner)
    forward = near(tok.at[twin], tok.at[twin], tok_send.at[2], tok_recv.at[2], partner)
    cache_copies = []
    for group, owner in enumerate((partner, diag)):
        for at, (hbm, buf) in enumerate(((keys_hbm, kc), (values_hbm, vc))):
            cache_copies.append(
                near(
                    hbm.at[0, :, cols(owner, width)],
                    buf.at[group, core],
                    cache_send.at[2 * group + at],
                    cache_recv.at[2 * group + at],
                    partner,
                )
            )
    if gather:
        weight_twin = near(
            out_weight_hbm, wo.at[1, :, cols(dp, piece)], x_sem.at[0], x_sem.at[1], twin
        )
        z, y = dp // ROW, dp % ROW
        has_up, has_down = z < LINE - 1, z > 0
        above = jnp.minimum(dp + ROW, DP - 1)
        below = jnp.maximum(dp - ROW, 0)
        beside = dp + 1 - 2 * y

        def carry(part, slot, origin, device):
            at = wo.at[part, :, cols(origin, piece)]
            return remote(at, at, w_send.at[part, slot], w_recv.at[part, slot], {"dp": device})

        def up(part, j):
            return carry(part, j, jnp.maximum(dp - ROW * j, 0), above)

        def down(part, j):
            return carry(part, LINE - 1 + j, jnp.minimum(dp + ROW * j, DP - 1), below)

        def across(part, j):
            return carry(part, 2 * LINE - 2 + j, (dp + DP - ROW * j) % DP, beside)

        def skip(part):
            first = jnp.where(z == LINE - 1, y, dp)
            return carry(part, 3 * LINE - 2, dp, first)

        def step_up(part, j):
            @pl.when(z >= j)
            def _():
                up(part, j - 1).wait_recv()
                if j < LINE - 1:
                    pl.when(has_up)(lambda: up(part, j).start())
                across(part, j).start()

        def step_down(part, j):
            @pl.when(z + j < LINE)
            def _():
                if j < LINE - 1:
                    down(part, j - 1).wait_recv()
                else:
                    skip(part).wait_recv()
                if j < LINE - 2:
                    pl.when(has_down)(lambda: down(part, j).start())
                across(part, LINE - j).start()

        def begin_down(part):
            pl.when(has_down)(lambda: down(part, 0).start())
            pl.when(z == LINE - 1)(lambda: skip(part).start())
            pl.when(y == 1)(lambda: across(part, 0).start())

        def begin_up(part):
            pl.when(has_up)(lambda: up(part, 0).start())
            pl.when(y == 0)(lambda: across(part, 0).start())

    def steps(*moves):
        def move():
            for part, j, *way in moves:
                if way != [DOWN]:
                    step_up(part, j)
                if way != [UP]:
                    step_down(part, j)

        return move if gather else nothing

    barrier = pltpu.get_barrier_semaphore()

    def tell(sem, index):
        pl.semaphore_signal(sem, inc=1, device_id={"seq": index}, device_id_type=MESH)

    @pl.when(me == 1)
    def _():
        tell(barrier, 0)
        tell(barrier, 3)

    @pl.when(me == 3)
    def _():
        tell(barrier, 2)

    @pl.when(me != 1)
    def _():
        pl.semaphore_wait(barrier, 1 + (me == 2).astype(jnp.int32))

    @pl.when(me == 0)
    def _():
        tell(barrier, 2)
        tell(ready.at[0], 1)

    @pl.when(me == 2)
    def _():
        tell(ready.at[2], 0)
        tell(ready.at[2], 1)
        tell(ready.at[2], 3)

    @pl.when(me == 3)
    def _():
        tell(ready.at[3], 1)

    def cross():
        if gather:
            weight_twin.start()
        to_twin.start()

    @pl.when(chip == 1)
    def _():
        cross()

    @pl.when(me == 1)
    def _():
        pl.semaphore_wait(ready.at[0], 1)

    @pl.when(me == 3)
    def _():
        pl.semaphore_wait(ready.at[2], 1)

    to_partner.start()
    for copy in cache_copies:
        copy.start()

    @pl.when(me == 0)
    def _():
        pl.semaphore_wait(ready.at[2], 1)

    @pl.when(me == 1)
    def _():
        pl.semaphore_wait(ready.at[3], 1)

    @pl.when(chip == 0)
    def _():
        cross()

    @pl.when(me == LEADER)
    def _():
        pl.semaphore_wait(ready.at[2], 1)

    def tell_far(sem, index):
        pl.semaphore_signal(sem, inc=1, device_id={"dp": index}, device_id_type=MESH)

    def spread_word(sem):
        @pl.when(me == LEADER)
        def _():
            for index in (0, 2, 3):
                tell(sem, index)

        @pl.when(me != LEADER)
        def _():
            pl.semaphore_wait(sem, 1)

    if gather:
        @pl.when(me == LEADER)
        def _():
            @pl.when(z + y > 0)
            def _():
                pl.semaphore_wait(barrier, has_down.astype(jnp.int32) + y)

            pl.when(has_up)(lambda: tell_far(barrier, above))
            pl.when(y == 0)(lambda: tell_far(barrier, beside))
            pl.when(has_down)(lambda: tell_far(up_sem.at[0], below))
            pl.when(y == 1)(lambda: tell_far(up_sem.at[1], beside))

        spread_word(far_ready.at[0])
        out_copies[0].wait()
        begin_down(0)

    def far_begin():
        @pl.when(me == LEADER)
        def _():
            pl.when(has_up)(lambda: pl.semaphore_wait(up_sem.at[0], 1))
            pl.when(y == 0)(lambda: pl.semaphore_wait(up_sem.at[1], 1))

        spread_word(far_ready.at[1])
        begin_up(0)

        @pl.when(z + y == 0)
        def _():
            weight_twin.wait_recv()

        begin_up(1)

    def far_early():
        @pl.when(z + y > 0)
        def _():
            weight_twin.wait_recv()
            begin_down(1)

    bias = bias_ref[:, cols(me, 3 * width)]
    low = lanes(rows) < HEAD_DIM
    ones = jnp.ones((rows, LANES), BF16)
    none = jnp.zeros((rows, LANES), BF16)

    def markers(count):
        lane = lanes(count)
        return (jnp.where(lane == at, 1.0, 0.0).astype(BF16) for at in (HEAD_DIM, 0))

    middle, first = markers(rows)

    def project(block):
        inputs = tok[block]
        side_, here_ = block // 2, rows_of(block % 2, rows)
        at = rows_of(old // rows + block, rows)
        for pair in range(heads // 2):
            here = slice(6 * pair * HEAD_DIM, 6 * (pair + 1) * HEAD_DIM)
            summed = jnp.dot(inputs, weight[:, here], preferred_element_type=F32) + bias[:, here]
            a, b, c = (summed[:, i * LANES : (i + 1) * LANES] for i in range(3))
            query = (jnp.where(low, a, b).astype(BF16).astype(F32) * HEAD_DIM**-0.5).astype(BF16)
            key = pltpu.roll(jnp.where(low, c, a), HEAD_DIM, 1).astype(BF16)
            value = jnp.where(low, b, c).astype(BF16)
            qo[block, :, pair * LANES : (pair + 1) * LANES] = query
            even, odd = split(query, middle, first)
            q0[side_, 2 * pair, here_], q0[side_, 2 * pair + 1, here_] = even, odd
            k0[2 * pair, at], k0[2 * pair + 1, at] = split(key, none, none)
            v0[2 * pair, at], v0[2 * pair + 1, at] = split(value, ones, ones)

    def query_copy(block):
        return near(qo.at[block], qt.at[block], q_send.at[block], q_recv.at[block], twin)

    def prepare(group, keys, values):
        lane_ = lanes(cache_rows)
        for c in range(2):
            place = lax.broadcasted_iota(jnp.int32, (cache_rows, LANES), 0)
            live = (2 * chip + c) * cache_rows + place < cached
            scale = jnp.where(live, 1.0, 0.0).astype(BF16)
            cap = jnp.where(live, 0.0, DEAD)
            cap_even = jnp.where(lane_ == HEAD_DIM, cap, 0.0).astype(BF16)
            cap_odd = jnp.where(lane_ == 0, cap, 0.0).astype(BF16)
            full = jnp.ones((cache_rows, LANES), BF16)
            at = slice(c * cache_rows, (c + 1) * cache_rows)
            for pair in range(heads // 2):
                here = slice(pair * LANES, (pair + 1) * LANES)
                key = kc[group, c, :, here] * scale
                keys[2 * pair, at], keys[2 * pair + 1, at] = split(key, cap_even, cap_odd)
                value = vc[group, c, :, here]
                values[2 * pair, at], values[2 * pair + 1, at] = split(value, full, full)

    def cached_keys(keys, values):
        return (lambda h: keys[h, 0:old]), (lambda h: values[h, 0:old])

    def new_keys(start, count):
        at = rows_of(old // half + start, half) if count == half else pl.ds(old, count)
        return (lambda h: k0[h, at]), (lambda h: v0[h, at])

    def own_heads(side_, fresh, cap, between=()):
        parts = [cached_keys(k0, v0), fresh]
        return attend(
            heads,
            lambda h: q0[side_, h],
            [k for k, _ in parts],
            [v for _, v in parts],
            [None, cap],
            between,
        )

    def twin_heads(side_, between=()):
        marks = list(markers(half))
        queries = []
        both = qt[pl.ds(2 * side_, 2)].reshape(half, width)
        for pair in range(heads // 2):
            queries.extend(split(both[:, pair * LANES : (pair + 1) * LANES], *marks))
        k, v = cached_keys(k1, v1)
        return attend(heads, lambda h: queries[h], [k], [v], [None], between)

    def part_copy(group, block):
        return near(
            part_send.at[group, block],
            part_recv.at[1 - group, block],
            p_send.at[group, block],
            p_recv.at[1 - group, block],
            twin,
        )

    def stat_copy(group):
        return near(
            stat_send.at[group],
            stat_recv.at[1 - group],
            s_sem.at[0, group],
            s_sem.at[1, 1 - group],
            twin,
        )

    locals_[0].wait()
    locals_[1].wait()
    project(me)
    to_partner.wait_recv()
    project(partner)

    row = lax.broadcasted_iota(jnp.int32, (half, half), 0)
    new = lax.broadcasted_iota(jnp.int32, (half, half), 1)
    near_cap[...] = jnp.where((new <= row) & (chip * half + new < filled), LIVE, DEAD)
    row = (1 - chip) * half + lax.broadcasted_iota(jnp.int32, (half, new_rows), 0)
    new = lax.broadcasted_iota(jnp.int32, (half, new_rows), 1)
    caps[...] = jnp.where((new <= row) & (new < filled), LIVE, DEAD)
    for at in (0, 1):
        locals_[2 + at].wait()
        cache_copies[at].wait_recv()
    prepare(0, k0, v0)
    query_copy(me).start()
    query_copy(partner).start()
    if gather:
        far_early()
    tops, products = own_heads(
        chip, new_keys(chip, half), near_cap[...], [nothing, far_begin if gather else nothing]
    )
    for h in range(heads):
        own_top[h] = jnp.broadcast_to(tops[h], (half, LANES))
        own_product[h] = products[h]
    for at in (2, 3):
        locals_[2 + at].wait()
        cache_copies[at].wait_recv()
    prepare(1, k1, v1)
    steps((0, 1), (1, 1))()

    to_twin.wait_recv()
    forward.start()
    project(twin)
    query_copy(twin).start()
    forward.wait_recv()
    project(diag)
    query_copy(diag).start()

    def send_part(group, tops, products):
        parts, stat = finish(tops, products)
        stat_send[group] = jnp.concatenate([stat[:rows].T[0:8], stat[rows:].T[0:8]], 1)
        stat_copy(group).start()
        for pair in range(heads // 2):
            both = parts[pair].astype(BF16)
            for block in range(2):
                part_send[group, block, :, pair * LANES : (pair + 1) * LANES] = both[
                    block * rows : (block + 1) * rows
                ]
        for block in (1 - core, core):
            part_copy(group, block).start()

    def keep_part(group, tops, products):
        parts, stat = finish(tops, products)
        for pair in range(heads // 2):
            at = slice(pair * LANES, (pair + 1) * LANES)
            keep[group, :, :, at] = parts[pair].reshape(2, rows, LANES)
        keep_stat[group] = stat

    query_copy(twin).wait_recv()
    query_copy(diag).wait_recv()
    send_part(1, *twin_heads(1 - chip, [steps((0, 2)), nothing, steps((1, 2), (0, 3, DOWN))]))
    send_part(0, *own_heads(1 - chip, new_keys(0, new_rows), caps[...]))
    steps((1, 3, DOWN), (0, 3, UP))()

    @pl.when(chip == 1)
    def _():
        fresh = lax.broadcasted_iota(jnp.int32, (1, half), 1) < filled
        k, v = new_keys(0, half)
        tops, products = attend(
            heads, lambda h: q0[1, h], [k], [v], [jnp.where(fresh, LIVE, DEAD)]
        )
        for h in range(heads):
            before = own_top[h]
            top = jnp.maximum(before, tops[h])
            own_product[h] = own_product[h] * jnp.exp(before - top) + products[h] * jnp.exp(
                tops[h] - top
            )
            own_top[h] = top

    keep_part(0, [own_top[h] for h in range(heads)], [own_product[h] for h in range(heads)])
    query_copy(me).wait_recv()
    query_copy(partner).wait_recv()
    keep_part(1, *twin_heads(chip, [nothing, steps((1, 3, UP))]))

    for copy in out_copies if not gather else []:
        copy.wait()
    def weights_there(part):
        if gather:
            for j in range(LINE):
                across(part, j).wait_recv()

    def weigh(group):
        stat_copy(1 - group).wait_recv()
        filler = jnp.zeros((LANES - 8, half), F32)
        other = jnp.concatenate([stat_recv[group], filler], 0).T
        share = 1.0 / (1.0 + jnp.exp(other - keep_stat[group]))
        wide = spread(share, heads).reshape(2, rows, width)
        keep[group] = keep[group] * wide
        rest[group] = 1.0 - wide

    def combine(group, block):
        attn = keep[group, block] + rest[group, block] * part_recv[group, block].astype(F32)
        return jnp.dot(attn.astype(BF16), wo[group], preferred_element_type=F32)

    mixed_copy = near(mixed_send, mixed_recv, m_sem.at[0], m_sem.at[1], partner)
    weigh(0)
    weigh(1)
    weights_there(0)
    for block in range(2):
        part_copy(1, block).wait_recv()
        mixed_sum[block] = combine(0, block)
    mixed_sum[core] = mixed_sum[core] + out_bias_ref[...] + tok[me].astype(F32)
    weights_there(1)
    part_copy(0, 1 - core).wait_recv()
    mixed_send[...] = (mixed_sum[1 - core] + combine(1, 1 - core)).astype(BF16)
    mixed_copy.start()
    part_copy(0, core).wait_recv()
    mixed = mixed_sum[core] + combine(1, core)
    mixed_copy.wait_recv()
    mixed = mixed + mixed_recv[...].astype(F32)
    center = mixed - jnp.mean(mixed, axis=1, keepdims=True)
    variance = jnp.mean(center * center, axis=1, keepdims=True)
    normed = center * lax.rsqrt(variance + 1e-05) * gain_ref[...] + shift_ref[...]
    out_ref[0] = normed.astype(BF16)

    sent = [to_partner, forward, stat_copy(0), stat_copy(1), mixed_copy] + cache_copies
    sent += [to_twin] + [query_copy(b) for b in range(tok.shape[0])]
    sent += [part_copy(g, b) for g in range(2) for b in range(2)]
    if gather:
        sent.append(weight_twin)
        for part in range(2):
            sent += [across(part, j) for j in range(LINE)]
            for j in range(LINE - 1):
                pl.when(has_up & (z >= j))(up(part, j).wait_send)
                if j < LINE - 2:
                    pl.when(has_down & (z + j < LINE))(down(part, j).wait_send)
            pl.when(z == LINE - 1)(skip(part).wait_send)
    for copy in sent:
        copy.wait_send()


def local(
    tokens,
    cache_keys,
    cache_values,
    qkv_weight,
    qkv_bias,
    out_weight,
    out_bias,
    norm_gain,
    norm_bias,
    cached_len,
    span_len,
    slot_request,
):
    rows, model = tokens.shape[1:]
    cache_rows = cache_keys.shape[1]
    width = qkv_weight.shape[1] // 3
    heads = width // HEAD_DIM
    blocks = lax.axis_size("seq")
    half = 2 * rows
    old = 2 * cache_rows
    total = old + blocks * rows
    hbm = pl.BlockSpec(memory_space=pltpu.HBM)
    vmem = pl.BlockSpec(memory_space=pltpu.VMEM)
    smem = pl.BlockSpec(memory_space=pltpu.SMEM)
    dma = pltpu.SemaphoreType.DMA

    gather = lax.axis_size("dp") == DP and out_weight.shape[1] % 128 == 0
    if not gather:
        out_weight = lax.all_gather(out_weight, "dp", axis=1, tiled=True)
        out_weight = lax.all_gather(out_weight, "seq", axis=0)

    return pl.pallas_call(
        functools.partial(kernel, gather),
        out_shape=pltpu.VMEM((1, rows, model), BF16),
        in_specs=[smem] * 3 + [hbm] * 5 + [vmem] * 4,
        out_specs=vmem,
        scratch_shapes=[
            pltpu.VMEM((blocks, rows, model), BF16),
            pltpu.VMEM((model, 3 * width), BF16),
            pltpu.VMEM((2, 2, cache_rows, width), BF16),
            pltpu.VMEM((2, 2, cache_rows, width), BF16),
            pltpu.VMEM((heads, total, LANES), BF16),
            pltpu.VMEM((heads, total, LANES), BF16),
            pltpu.VMEM((heads, old, LANES), BF16),
            pltpu.VMEM((heads, old, LANES), BF16),
            pltpu.VMEM((2, heads, half, LANES), BF16),
            pltpu.VMEM((blocks, rows, width), BF16),
            pltpu.VMEM((blocks, rows, width), BF16),
            pltpu.VMEM((half, half), F32),
            pltpu.VMEM((half, blocks * rows), F32),
            pltpu.VMEM((heads, half, LANES), F32),
            pltpu.VMEM((heads, half, LANES), F32),
            pltpu.VMEM((2, 2, rows, width), F32),
            pltpu.VMEM((2, half, LANES), F32),
            pltpu.VMEM((2, 2, rows, width), F32),
            pltpu.VMEM((2, rows, model), F32),
            pltpu.VMEM((2, 2, rows, width), BF16),
            pltpu.VMEM((2, 2, rows, width), BF16),
            pltpu.VMEM((2, 8, half), F32),
            pltpu.VMEM((2, 8, half), F32),
            pltpu.VMEM((rows, model), BF16),
            pltpu.VMEM((rows, model), BF16),
            pltpu.VMEM((2, width, model), BF16),
            dma((8,)),
            dma((3,)),
            dma((3,)),
            dma((4,)),
            dma((4,)),
            dma((blocks,)),
            dma((blocks,)),
            dma((2, 2)),
            dma((2, 2)),
            dma((2, 2)),
            dma((2,)),
            dma((2,)),
            dma((2, 3 * LINE - 1)),
            dma((2, 3 * LINE - 1)),
            pltpu.SemaphoreType.REGULAR((4,)),
            pltpu.SemaphoreType.REGULAR((2,)),
            pltpu.SemaphoreType.REGULAR((2,)),
        ],
        compiler_params=pltpu.CompilerParams(
            collective_id=0, has_side_effects=True, vmem_limit_bytes=60 << 20
        ),
        cost_estimate=pl.CostEstimate(
            flops=6_000_000_000, bytes_accessed=6_000_000, transcendentals=5_000_000
        ),
        name="sublayer",
    )(
        cached_len,
        span_len,
        slot_request,
        tokens,
        cache_keys,
        cache_values,
        qkv_weight,
        out_weight,
        qkv_bias.reshape(1, -1),
        out_bias.reshape(1, -1),
        norm_gain.reshape(1, -1),
        norm_bias.reshape(1, -1),
    )


def solution(mesh):
    return jax.shard_map(
        local,
        mesh=mesh,
        in_specs=(
            P("dp", "seq", None),
            P("dp", "seq", None),
            P("dp", "seq", None),
            P(None, "seq"),
            P(),
            P("seq", "dp"),
            P(),
            P(),
            P(),
            P(),
            P(),
            P(),
        ),
        out_specs=P("dp", "seq", None),
        check_vma=False,
    )
```

```python
import functools

import jax
import jax.numpy as jnp
from jax import lax
from jax.experimental import pallas as pl
from jax.experimental.pallas import tpu as pltpu
from jax.sharding import PartitionSpec as P

HEAD_DIM = 64
LANES = 128
LIVE = 3e38
DEAD = -1e30
F32 = jnp.float32
BF16 = jnp.bfloat16
MESH = pl.DeviceIdType.MESH
LEADER = 1
DP = 8
ROW = 2
LINE = DP // ROW
UP, DOWN = 1, 2


def nothing():
    pass


def peers():
    me = lax.axis_index("seq")
    core = me % 2
    partner = me + 1 - 2 * core
    twin = (me + 2) % 4
    diag = (partner + 2) % 4
    return me, core, partner, twin, diag


def cols(index, width):
    return pl.ds(pl.multiple_of(index * width, 128), width)


def rows_of(index, height):
    return pl.ds(pl.multiple_of(index * height, 128), height)


def nt(a, b):
    return lax.dot_general(a, b, (((1,), (1,)), ((), ())), preferred_element_type=F32)


def lanes(rows):
    return lax.broadcasted_iota(jnp.int32, (rows, LANES), 1)


def split(pair, even, odd):
    low = lanes(pair.shape[0]) < HEAD_DIM
    return jnp.where(low, pair, even), jnp.where(low, odd, pair)


def attend(heads, query, keys, values, caps, between=()):
    def scores(h):
        out = []
        for k, cap in zip(keys, caps):
            s = nt(query(h), k(h))
            out.append(s if cap is None else jnp.minimum(s, cap))
        return out

    now = scores(0)
    tops, products = [], []
    for h in range(heads):
        later = scores(h + 1) if h + 1 < heads else None
        top = functools.reduce(jnp.maximum, [jnp.max(s, 1, keepdims=True) for s in now])
        product = 0.0
        for s, v in zip(now, values):
            product = product + jnp.dot(
                jnp.exp(s - top).astype(BF16), v(h), preferred_element_type=F32
            )
        tops.append(top)
        products.append(product)
        now = later
        if h < len(between):
            between[h]()
    return tops, products


def finish(tops, products):
    rows = products[0].shape[0]
    lane = lanes(rows)
    low = lane < HEAD_DIM
    parts = []
    left = jnp.zeros((rows, LANES), F32)
    right = jnp.zeros((rows, LANES), F32)
    for pair in range(len(products) // 2):
        a, b = products[2 * pair], products[2 * pair + 1]
        total = jnp.where(low, b, a)
        log = jnp.log(total)
        right = jnp.where(lane == HEAD_DIM + 2 * pair, tops[2 * pair] + log, right)
        left = jnp.where(lane == 2 * pair + 1, tops[2 * pair + 1] + log, left)
        parts.append(jnp.where(low, a, b) / pltpu.roll(total, HEAD_DIM, 1))
    return parts, left + pltpu.roll(right, HEAD_DIM, 1)


def spread(tile, heads):
    low = lanes(tile.shape[0]) < HEAD_DIM
    out = []
    for at in range(0, heads, 2):
        out.append(jnp.where(low, tile[:, at : at + 1], tile[:, at + 1 : at + 2]))
    return jnp.concatenate(out, 1)


def kernel(
    gather,
    cached_hbm,
    span_hbm,
    slot_hbm,
    tokens_hbm,
    keys_hbm,
    values_hbm,
    weight_hbm,
    out_weight_hbm,
    bias_hbm,
    out_bias_hbm,
    gain_hbm,
    shift_hbm,
    out_ref,
    cached_ref,
    span_ref,
    slot_ref,
    bias_ref,
    out_bias_ref,
    gain_ref,
    shift_ref,
    small_sem,
    tok,
    weight,
    kc,
    vc,
    k0,
    v0,
    k1,
    v1,
    q0,
    qo,
    qt,
    near_cap,
    caps,
    own_top,
    own_product,
    keep,
    keep_stat,
    rest,
    mixed_sum,
    part_send,
    part_recv,
    stat_send,
    stat_recv,
    mixed_send,
    mixed_recv,
    wo,
    local_sem,
    tok_send,
    tok_recv,
    cache_send,
    cache_recv,
    q_send,
    q_recv,
    p_send,
    p_recv,
    s_sem,
    m_sem,
    x_sem,
    w_send,
    w_recv,
    ready,
    up_sem,
    far_ready,
):
    me, core, partner, twin, diag = peers()
    chip = me // 2
    rows = tok.shape[1]
    half = 2 * rows
    cache_rows = kc.shape[2]
    old = 2 * cache_rows
    width = kc.shape[3]
    heads = width // HEAD_DIM
    dp = lax.axis_index("dp")
    new_rows = tok.shape[0] * rows

    small = [
        pltpu.make_async_copy(hbm, ref, small_sem.at[at])
        for at, (hbm, ref) in enumerate(
            (
                (bias_hbm, bias_ref),
                (cached_hbm, cached_ref),
                (span_hbm, span_ref),
                (slot_hbm, slot_ref),
                (out_bias_hbm, out_bias_ref),
                (gain_hbm, gain_ref),
                (shift_hbm, shift_ref),
            )
        )
    ]
    locals_ = [
        pltpu.make_async_copy(tokens_hbm.at[0], tok.at[me], local_sem.at[0]),
        pltpu.make_async_copy(weight_hbm, weight, local_sem.at[1]),
    ]
    for group, owner in enumerate((me, twin)):
        for at, (hbm, buf) in enumerate(((keys_hbm, kc), (values_hbm, vc))):
            locals_.append(
                pltpu.make_async_copy(
                    hbm.at[0, :, cols(owner, width)],
                    buf.at[group, core],
                    local_sem.at[2 + 2 * group + at],
                )
            )
    if gather:
        piece = out_weight_hbm.shape[1]
        out_copies = [
            pltpu.make_async_copy(out_weight_hbm, wo.at[0, :, cols(dp, piece)], local_sem.at[6])
        ]
    else:
        out_copies = [
            pltpu.make_async_copy(out_weight_hbm.at[owner], wo.at[at], local_sem.at[6 + at])
            for at, owner in enumerate((me, twin))
        ]

    def remote(src, dst, send, recv, device):
        return pltpu.make_async_remote_copy(
            src_ref=src,
            dst_ref=dst,
            send_sem=send,
            recv_sem=recv,
            device_id=device,
            device_id_type=MESH,
        )

    def near(src, dst, send, recv, index):
        return remote(src, dst, send, recv, {"seq": index})

    to_twin = near(tokens_hbm.at[0], tok.at[me], tok_send.at[1], tok_recv.at[1], twin)
    to_partner = near(tokens_hbm.at[0], tok.at[me], tok_send.at[0], tok_recv.at[0], partner)
    forward = near(tok.at[twin], tok.at[twin], tok_send.at[2], tok_recv.at[2], partner)
    cache_copies = []
    for group, owner in enumerate((partner, diag)):
        for at, (hbm, buf) in enumerate(((keys_hbm, kc), (values_hbm, vc))):
            cache_copies.append(
                near(
                    hbm.at[0, :, cols(owner, width)],
                    buf.at[group, core],
                    cache_send.at[2 * group + at],
                    cache_recv.at[2 * group + at],
                    partner,
                )
            )
    if gather:
        weight_twin = near(
            out_weight_hbm, wo.at[1, :, cols(dp, piece)], x_sem.at[0], x_sem.at[1], twin
        )
        z, y = dp // ROW, dp % ROW
        has_up, has_down = z < LINE - 1, z > 0
        above = jnp.minimum(dp + ROW, DP - 1)
        below = jnp.maximum(dp - ROW, 0)
        beside = dp + 1 - 2 * y

        def carry(part, slot, origin, device):
            at = wo.at[part, :, cols(origin, piece)]
            return remote(at, at, w_send.at[part, slot], w_recv.at[part, slot], {"dp": device})

        def up(part, j):
            return carry(part, j, jnp.maximum(dp - ROW * j, 0), above)

        def down(part, j):
            return carry(part, LINE - 1 + j, jnp.minimum(dp + ROW * j, DP - 1), below)

        def across(part, j):
            return carry(part, 2 * LINE - 2 + j, (dp + DP - ROW * j) % DP, beside)

        def skip(part):
            first = jnp.where(z == LINE - 1, y, dp)
            return carry(part, 3 * LINE - 2, dp, first)

        def step_up(part, j):
            @pl.when(z >= j)
            def _():
                up(part, j - 1).wait_recv()
                if j < LINE - 1:
                    pl.when(has_up)(lambda: up(part, j).start())
                across(part, j).start()

        def step_down(part, j):
            @pl.when(z + j < LINE)
            def _():
                if j < LINE - 1:
                    down(part, j - 1).wait_recv()
                else:
                    skip(part).wait_recv()
                if j < LINE - 2:
                    pl.when(has_down)(lambda: down(part, j).start())
                across(part, LINE - j).start()

        def begin_down(part):
            pl.when(has_down)(lambda: down(part, 0).start())
            pl.when(z == LINE - 1)(lambda: skip(part).start())
            pl.when(y == 1)(lambda: across(part, 0).start())

        def begin_up(part):
            pl.when(has_up)(lambda: up(part, 0).start())
            pl.when(y == 0)(lambda: across(part, 0).start())

    def steps(*moves):
        def move():
            for part, j, *way in moves:
                if way != [DOWN]:
                    step_up(part, j)
                if way != [UP]:
                    step_down(part, j)

        return move if gather else nothing

    barrier = pltpu.get_barrier_semaphore()

    def tell(sem, index):
        pl.semaphore_signal(sem, inc=1, device_id={"seq": index}, device_id_type=MESH)

    @pl.when(me == 1)
    def _():
        tell(barrier, 0)
        tell(barrier, 3)

    @pl.when(me == 3)
    def _():
        tell(barrier, 2)

    @pl.when(me != 1)
    def _():
        pl.semaphore_wait(barrier, 1 + (me == 2).astype(jnp.int32))

    @pl.when(me == 0)
    def _():
        tell(barrier, 2)
        tell(ready.at[0], 1)

    @pl.when(me == 2)
    def _():
        tell(ready.at[2], 0)
        tell(ready.at[2], 1)
        tell(ready.at[2], 3)

    @pl.when(me == 3)
    def _():
        tell(ready.at[3], 1)

    def cross():
        if gather:
            weight_twin.start()
        to_twin.start()

    @pl.when(chip == 1)
    def _():
        cross()

    for copy in locals_ + out_copies + small:
        copy.start()

    @pl.when(me == 1)
    def _():
        pl.semaphore_wait(ready.at[0], 1)

    @pl.when(me == 3)
    def _():
        pl.semaphore_wait(ready.at[2], 1)

    to_partner.start()
    for copy in cache_copies:
        copy.start()

    @pl.when(me == 0)
    def _():
        pl.semaphore_wait(ready.at[2], 1)

    @pl.when(me == 1)
    def _():
        pl.semaphore_wait(ready.at[3], 1)

    @pl.when(chip == 0)
    def _():
        cross()

    @pl.when(me == LEADER)
    def _():
        pl.semaphore_wait(ready.at[2], 1)

    def tell_far(sem, index):
        pl.semaphore_signal(sem, inc=1, device_id={"dp": index}, device_id_type=MESH)

    def spread_word(sem):
        @pl.when(me == LEADER)
        def _():
            for index in (0, 2, 3):
                tell(sem, index)

        @pl.when(me != LEADER)
        def _():
            pl.semaphore_wait(sem, 1)

    if gather:
        @pl.when(me == LEADER)
        def _():
            @pl.when(z + y > 0)
            def _():
                pl.semaphore_wait(barrier, has_down.astype(jnp.int32) + y)

            pl.when(has_up)(lambda: tell_far(barrier, above))
            pl.when(y == 0)(lambda: tell_far(barrier, beside))
            pl.when(has_down)(lambda: tell_far(up_sem.at[0], below))
            pl.when(y == 1)(lambda: tell_far(up_sem.at[1], beside))

        spread_word(far_ready.at[0])
        out_copies[0].wait()
        begin_down(0)

    def far_begin():
        @pl.when(me == LEADER)
        def _():
            pl.when(has_up)(lambda: pl.semaphore_wait(up_sem.at[0], 1))
            pl.when(y == 0)(lambda: pl.semaphore_wait(up_sem.at[1], 1))

        spread_word(far_ready.at[1])
        begin_up(0)

        @pl.when(z + y == 0)
        def _():
            weight_twin.wait_recv()

        begin_up(1)

    def far_early():
        @pl.when(z + y > 0)
        def _():
            weight_twin.wait_recv()
            begin_down(1)

    for copy in small:
        copy.wait()
    request = slot_ref[dp]
    cached = cached_ref[request]
    filled = span_ref[request]
    bias = bias_ref[:, cols(me, 3 * width)]
    low = lanes(rows) < HEAD_DIM
    ones = jnp.ones((rows, LANES), BF16)
    none = jnp.zeros((rows, LANES), BF16)

    def markers(count):
        lane = lanes(count)
        return (jnp.where(lane == at, 1.0, 0.0).astype(BF16) for at in (HEAD_DIM, 0))

    middle, first = markers(rows)

    def project(block):
        inputs = tok[block]
        side_, here_ = block // 2, rows_of(block % 2, rows)
        at = rows_of(old // rows + block, rows)
        for pair in range(heads // 2):
            here = slice(6 * pair * HEAD_DIM, 6 * (pair + 1) * HEAD_DIM)
            summed = jnp.dot(inputs, weight[:, here], preferred_element_type=F32) + bias[:, here]
            a, b, c = (summed[:, i * LANES : (i + 1) * LANES] for i in range(3))
            query = (jnp.where(low, a, b).astype(BF16).astype(F32) * HEAD_DIM**-0.5).astype(BF16)
            key = pltpu.roll(jnp.where(low, c, a), HEAD_DIM, 1).astype(BF16)
            value = jnp.where(low, b, c).astype(BF16)
            qo[block, :, pair * LANES : (pair + 1) * LANES] = query
            even, odd = split(query, middle, first)
            q0[side_, 2 * pair, here_], q0[side_, 2 * pair + 1, here_] = even, odd
            k0[2 * pair, at], k0[2 * pair + 1, at] = split(key, none, none)
            v0[2 * pair, at], v0[2 * pair + 1, at] = split(value, ones, ones)

    def query_copy(block):
        return near(qo.at[block], qt.at[block], q_send.at[block], q_recv.at[block], twin)

    def prepare(group, keys, values):
        lane_ = lanes(cache_rows)
        for c in range(2):
            place = lax.broadcasted_iota(jnp.int32, (cache_rows, LANES), 0)
            live = (2 * chip + c) * cache_rows + place < cached
            scale = jnp.where(live, 1.0, 0.0).astype(BF16)
            cap = jnp.where(live, 0.0, DEAD)
            cap_even = jnp.where(lane_ == HEAD_DIM, cap, 0.0).astype(BF16)
            cap_odd = jnp.where(lane_ == 0, cap, 0.0).astype(BF16)
            full = jnp.ones((cache_rows, LANES), BF16)
            at = slice(c * cache_rows, (c + 1) * cache_rows)
            for pair in range(heads // 2):
                here = slice(pair * LANES, (pair + 1) * LANES)
                key = kc[group, c, :, here] * scale
                keys[2 * pair, at], keys[2 * pair + 1, at] = split(key, cap_even, cap_odd)
                value = vc[group, c, :, here]
                values[2 * pair, at], values[2 * pair + 1, at] = split(value, full, full)

    def cached_keys(keys, values):
        return (lambda h: keys[h, 0:old]), (lambda h: values[h, 0:old])

    def new_keys(start, count):
        at = rows_of(old // half + start, half) if count == half else pl.ds(old, count)
        return (lambda h: k0[h, at]), (lambda h: v0[h, at])

    def own_heads(side_, fresh, cap, between=()):
        parts = [cached_keys(k0, v0), fresh]
        return attend(
            heads,
            lambda h: q0[side_, h],
            [k for k, _ in parts],
            [v for _, v in parts],
            [None, cap],
            between,
        )

    def twin_heads(side_, between=()):
        marks = list(markers(half))
        queries = []
        both = qt[pl.ds(2 * side_, 2)].reshape(half, width)
        for pair in range(heads // 2):
            queries.extend(split(both[:, pair * LANES : (pair + 1) * LANES], *marks))
        k, v = cached_keys(k1, v1)
        return attend(heads, lambda h: queries[h], [k], [v], [None], between)

    def part_copy(group, block):
        return near(
            part_send.at[group, block],
            part_recv.at[1 - group, block],
            p_send.at[group, block],
            p_recv.at[1 - group, block],
            twin,
        )

    def stat_copy(group):
        return near(
            stat_send.at[group],
            stat_recv.at[1 - group],
            s_sem.at[0, group],
            s_sem.at[1, 1 - group],
            twin,
        )

    locals_[0].wait()
    locals_[1].wait()
    project(me)
    to_partner.wait_recv()
    project(partner)

    row = lax.broadcasted_iota(jnp.int32, (half, half), 0)
    new = lax.broadcasted_iota(jnp.int32, (half, half), 1)
    near_cap[...] = jnp.where((new <= row) & (chip * half + new < filled), LIVE, DEAD)
    row = (1 - chip) * half + lax.broadcasted_iota(jnp.int32, (half, new_rows), 0)
    new = lax.broadcasted_iota(jnp.int32, (half, new_rows), 1)
    caps[...] = jnp.where((new <= row) & (new < filled), LIVE, DEAD)
    for at in (0, 1):
        locals_[2 + at].wait()
        cache_copies[at].wait_recv()
    prepare(0, k0, v0)
    query_copy(me).start()
    query_copy(partner).start()
    if gather:
        far_early()
    tops, products = own_heads(
        chip, new_keys(chip, half), near_cap[...], [nothing, far_begin if gather else nothing]
    )
    for h in range(heads):
        own_top[h] = jnp.broadcast_to(tops[h], (half, LANES))
        own_product[h] = products[h]
    for at in (2, 3):
        locals_[2 + at].wait()
        cache_copies[at].wait_recv()
    prepare(1, k1, v1)
    steps((0, 1), (1, 1))()

    to_twin.wait_recv()
    forward.start()
    project(twin)
    query_copy(twin).start()
    forward.wait_recv()
    project(diag)
    query_copy(diag).start()

    def send_part(group, tops, products):
        parts, stat = finish(tops, products)
        stat_send[group] = jnp.concatenate([stat[:rows].T[0:8], stat[rows:].T[0:8]], 1)
        stat_copy(group).start()
        for pair in range(heads // 2):
            both = parts[pair].astype(BF16)
            for block in range(2):
                part_send[group, block, :, pair * LANES : (pair + 1) * LANES] = both[
                    block * rows : (block + 1) * rows
                ]
        for block in (1 - core, core):
            part_copy(group, block).start()

    def keep_part(group, tops, products):
        parts, stat = finish(tops, products)
        for pair in range(heads // 2):
            at = slice(pair * LANES, (pair + 1) * LANES)
            keep[group, :, :, at] = parts[pair].reshape(2, rows, LANES)
        keep_stat[group] = stat

    query_copy(twin).wait_recv()
    query_copy(diag).wait_recv()
    send_part(1, *twin_heads(1 - chip, [steps((0, 2)), nothing, steps((1, 2), (0, 3, DOWN))]))
    send_part(0, *own_heads(1 - chip, new_keys(0, new_rows), caps[...]))
    steps((1, 3, DOWN), (0, 3, UP))()

    @pl.when(chip == 1)
    def _():
        fresh = lax.broadcasted_iota(jnp.int32, (1, half), 1) < filled
        k, v = new_keys(0, half)
        tops, products = attend(
            heads, lambda h: q0[1, h], [k], [v], [jnp.where(fresh, LIVE, DEAD)]
        )
        for h in range(heads):
            before = own_top[h]
            top = jnp.maximum(before, tops[h])
            own_product[h] = own_product[h] * jnp.exp(before - top) + products[h] * jnp.exp(
                tops[h] - top
            )
            own_top[h] = top

    keep_part(0, [own_top[h] for h in range(heads)], [own_product[h] for h in range(heads)])
    query_copy(me).wait_recv()
    query_copy(partner).wait_recv()
    keep_part(1, *twin_heads(chip, [nothing, steps((1, 3, UP))]))

    for copy in out_copies if not gather else []:
        copy.wait()
    def weights_there(part):
        if gather:
            for j in range(LINE):
                across(part, j).wait_recv()

    def weigh(group):
        stat_copy(1 - group).wait_recv()
        filler = jnp.zeros((LANES - 8, half), F32)
        other = jnp.concatenate([stat_recv[group], filler], 0).T
        share = 1.0 / (1.0 + jnp.exp(other - keep_stat[group]))
        wide = spread(share, heads).reshape(2, rows, width)
        keep[group] = keep[group] * wide
        rest[group] = 1.0 - wide

    def combine(group, block):
        attn = keep[group, block] + rest[group, block] * part_recv[group, block].astype(F32)
        return jnp.dot(attn.astype(BF16), wo[group], preferred_element_type=F32)

    mixed_copy = near(mixed_send, mixed_recv, m_sem.at[0], m_sem.at[1], partner)
    weigh(0)
    weigh(1)
    weights_there(0)
    for block in range(2):
        part_copy(1, block).wait_recv()
        mixed_sum[block] = combine(0, block)
    mixed_sum[core] = mixed_sum[core] + out_bias_ref[...] + tok[me].astype(F32)
    sent = [to_partner, to_twin, forward, stat_copy(0), stat_copy(1)] + cache_copies
    sent += [query_copy(b) for b in range(tok.shape[0])]
    sent += [part_copy(1, b) for b in range(2)]
    if gather:
        sent += [weight_twin] + [across(0, j) for j in range(LINE)]
        for part in range(2):
            for j in range(LINE - 1):
                pl.when(has_up & (z >= j))(up(part, j).wait_send)
                if j < LINE - 2:
                    pl.when(has_down & (z + j < LINE))(down(part, j).wait_send)
            pl.when(z == LINE - 1)(skip(part).wait_send)
    for copy in sent:
        copy.wait_send()
    weights_there(1)
    part_copy(0, 1 - core).wait_recv()
    mixed_send[...] = (mixed_sum[1 - core] + combine(1, 1 - core)).astype(BF16)
    mixed_copy.start()
    part_copy(0, core).wait_recv()
    mixed = mixed_sum[core] + combine(1, core)
    mixed_copy.wait_recv()
    mixed = mixed + mixed_recv[...].astype(F32)
    center = mixed - jnp.mean(mixed, axis=1, keepdims=True)
    variance = jnp.mean(center * center, axis=1, keepdims=True)
    normed = center * lax.rsqrt(variance + 1e-05) * gain_ref[...] + shift_ref[...]
    out_ref[0] = normed.astype(BF16)

    last = [part_copy(0, b) for b in range(2)] + [mixed_copy]
    if gather:
        last += [across(1, j) for j in range(LINE)]
    for copy in last:
        copy.wait_send()


def local(
    tokens,
    cache_keys,
    cache_values,
    qkv_weight,
    qkv_bias,
    out_weight,
    out_bias,
    norm_gain,
    norm_bias,
    cached_len,
    span_len,
    slot_request,
):
    rows, model = tokens.shape[1:]
    cache_rows = cache_keys.shape[1]
    width = qkv_weight.shape[1] // 3
    heads = width // HEAD_DIM
    blocks = lax.axis_size("seq")
    half = 2 * rows
    old = 2 * cache_rows
    total = old + blocks * rows
    hbm = pl.BlockSpec(memory_space=pltpu.HBM)
    vmem = pl.BlockSpec(memory_space=pltpu.VMEM)
    dma = pltpu.SemaphoreType.DMA

    gather = lax.axis_size("dp") == DP and out_weight.shape[1] % 128 == 0
    if not gather:
        out_weight = lax.all_gather(out_weight, "dp", axis=1, tiled=True)
        out_weight = lax.all_gather(out_weight, "seq", axis=0)

    return pl.pallas_call(
        functools.partial(kernel, gather),
        out_shape=pltpu.VMEM((1, rows, model), BF16),
        in_specs=[hbm] * 12,
        out_specs=vmem,
        scratch_shapes=[
            pltpu.SMEM(cached_len.shape, jnp.int32),
            pltpu.SMEM(span_len.shape, jnp.int32),
            pltpu.SMEM(slot_request.shape, jnp.int32),
            pltpu.VMEM((1, qkv_bias.size), F32),
            pltpu.VMEM((1, model), F32),
            pltpu.VMEM((1, model), F32),
            pltpu.VMEM((1, model), F32),
            dma((7,)),
            pltpu.VMEM((blocks, rows, model), BF16),
            pltpu.VMEM((model, 3 * width), BF16),
            pltpu.VMEM((2, 2, cache_rows, width), BF16),
            pltpu.VMEM((2, 2, cache_rows, width), BF16),
            pltpu.VMEM((heads, total, LANES), BF16),
            pltpu.VMEM((heads, total, LANES), BF16),
            pltpu.VMEM((heads, old, LANES), BF16),
            pltpu.VMEM((heads, old, LANES), BF16),
            pltpu.VMEM((2, heads, half, LANES), BF16),
            pltpu.VMEM((blocks, rows, width), BF16),
            pltpu.VMEM((blocks, rows, width), BF16),
            pltpu.VMEM((half, half), F32),
            pltpu.VMEM((half, blocks * rows), F32),
            pltpu.VMEM((heads, half, LANES), F32),
            pltpu.VMEM((heads, half, LANES), F32),
            pltpu.VMEM((2, 2, rows, width), F32),
            pltpu.VMEM((2, half, LANES), F32),
            pltpu.VMEM((2, 2, rows, width), F32),
            pltpu.VMEM((2, rows, model), F32),
            pltpu.VMEM((2, 2, rows, width), BF16),
            pltpu.VMEM((2, 2, rows, width), BF16),
            pltpu.VMEM((2, 8, half), F32),
            pltpu.VMEM((2, 8, half), F32),
            pltpu.VMEM((rows, model), BF16),
            pltpu.VMEM((rows, model), BF16),
            pltpu.VMEM((2, width, model), BF16),
            dma((8,)),
            dma((3,)),
            dma((3,)),
            dma((4,)),
            dma((4,)),
            dma((blocks,)),
            dma((blocks,)),
            dma((2, 2)),
            dma((2, 2)),
            dma((2, 2)),
            dma((2,)),
            dma((2,)),
            dma((2, 3 * LINE - 1)),
            dma((2, 3 * LINE - 1)),
            pltpu.SemaphoreType.REGULAR((4,)),
            pltpu.SemaphoreType.REGULAR((2,)),
            pltpu.SemaphoreType.REGULAR((2,)),
        ],
        compiler_params=pltpu.CompilerParams(
            collective_id=0, has_side_effects=True, vmem_limit_bytes=60 << 20
        ),
        cost_estimate=pl.CostEstimate(
            flops=6_000_000_000, bytes_accessed=6_000_000, transcendentals=5_000_000
        ),
        name="sublayer",
    )(
        cached_len,
        span_len,
        slot_request,
        tokens,
        cache_keys,
        cache_values,
        qkv_weight,
        out_weight,
        qkv_bias.reshape(1, -1),
        out_bias.reshape(1, -1),
        norm_gain.reshape(1, -1),
        norm_bias.reshape(1, -1),
    )


def solution(mesh):
    return jax.shard_map(
        local,
        mesh=mesh,
        in_specs=(
            P("dp", "seq", None),
            P("dp", "seq", None),
            P("dp", "seq", None),
            P(None, "seq"),
            P(),
            P("seq", "dp"),
            P(),
            P(),
            P(),
            P(),
            P(),
            P(),
        ),
        out_specs=P("dp", "seq", None),
        check_vma=False,
    )
```

```python
import functools

import jax
import jax.numpy as jnp
from jax import lax
from jax.experimental import pallas as pl
from jax.experimental.pallas import tpu as pltpu
from jax.sharding import PartitionSpec as P

HEAD_DIM = 64
LANES = 128
LIVE = 3e38
DEAD = -1e30
F32 = jnp.float32
BF16 = jnp.bfloat16
MESH = pl.DeviceIdType.MESH
LEADER = 1
DP = 8
ROW = 2
LINE = DP // ROW
UP, DOWN = 1, 2


def nothing():
    pass


def peers():
    me = lax.axis_index("seq")
    core = me % 2
    partner = me + 1 - 2 * core
    twin = (me + 2) % 4
    diag = (partner + 2) % 4
    return me, core, partner, twin, diag


def cols(index, width):
    return pl.ds(pl.multiple_of(index * width, 128), width)


def rows_of(index, height):
    return pl.ds(pl.multiple_of(index * height, 128), height)


def nt(a, b):
    return lax.dot_general(a, b, (((1,), (1,)), ((), ())), preferred_element_type=F32)


def lanes(rows):
    return lax.broadcasted_iota(jnp.int32, (rows, LANES), 1)


def split(pair, even, odd):
    low = lanes(pair.shape[0]) < HEAD_DIM
    return jnp.where(low, pair, even), jnp.where(low, odd, pair)


def attend(heads, query, keys, values, caps, between=()):
    def scores(h):
        out = []
        for k, cap in zip(keys, caps):
            s = nt(query(h), k(h))
            out.append(s if cap is None else jnp.minimum(s, cap))
        return out

    now = scores(0)
    tops, products = [], []
    for h in range(heads):
        later = scores(h + 1) if h + 1 < heads else None
        top = functools.reduce(jnp.maximum, [jnp.max(s, 1, keepdims=True) for s in now])
        product = 0.0
        for s, v in zip(now, values):
            product = product + jnp.dot(
                jnp.exp(s - top).astype(BF16), v(h), preferred_element_type=F32
            )
        tops.append(top)
        products.append(product)
        now = later
        if h < len(between):
            between[h]()
    return tops, products


def finish(tops, products):
    rows = products[0].shape[0]
    lane = lanes(rows)
    low = lane < HEAD_DIM
    parts = []
    left = jnp.zeros((rows, LANES), F32)
    right = jnp.zeros((rows, LANES), F32)
    for pair in range(len(products) // 2):
        a, b = products[2 * pair], products[2 * pair + 1]
        total = jnp.where(low, b, a)
        log = jnp.log(total)
        right = jnp.where(lane == HEAD_DIM + 2 * pair, tops[2 * pair] + log, right)
        left = jnp.where(lane == 2 * pair + 1, tops[2 * pair + 1] + log, left)
        parts.append(jnp.where(low, a, b) / pltpu.roll(total, HEAD_DIM, 1))
    return parts, left + pltpu.roll(right, HEAD_DIM, 1)


def spread(tile, heads):
    low = lanes(tile.shape[0]) < HEAD_DIM
    out = []
    for at in range(0, heads, 2):
        out.append(jnp.where(low, tile[:, at : at + 1], tile[:, at + 1 : at + 2]))
    return jnp.concatenate(out, 1)


def kernel(
    gather,
    cached_hbm,
    span_hbm,
    slot_hbm,
    tokens_hbm,
    keys_hbm,
    values_hbm,
    weight_hbm,
    out_weight_hbm,
    bias_hbm,
    out_bias_hbm,
    gain_hbm,
    shift_hbm,
    out_ref,
    cached_ref,
    span_ref,
    slot_ref,
    bias_ref,
    out_bias_ref,
    gain_ref,
    shift_ref,
    small_sem,
    tok,
    weight,
    kc,
    vc,
    k0,
    v0,
    k1,
    v1,
    q0,
    qo,
    qt,
    near_cap,
    caps,
    own_top,
    own_product,
    keep,
    keep_stat,
    rest,
    mixed_sum,
    part_send,
    part_recv,
    stat_send,
    stat_recv,
    mixed_send,
    mixed_recv,
    wo,
    local_sem,
    tok_send,
    tok_recv,
    cache_send,
    cache_recv,
    q_send,
    q_recv,
    p_send,
    p_recv,
    s_sem,
    m_sem,
    x_sem,
    w_send,
    w_recv,
    ready,
    up_sem,
    far_ready,
):
    me, core, partner, twin, diag = peers()
    chip = me // 2
    rows = tok.shape[1]
    half = 2 * rows
    cache_rows = kc.shape[2]
    old = 2 * cache_rows
    width = kc.shape[3]
    heads = width // HEAD_DIM
    dp = lax.axis_index("dp")
    new_rows = tok.shape[0] * rows

    small = [
        pltpu.make_async_copy(hbm, ref, small_sem.at[at])
        for at, (hbm, ref) in enumerate(
            (
                (bias_hbm, bias_ref),
                (cached_hbm, cached_ref),
                (span_hbm, span_ref),
                (slot_hbm, slot_ref),
                (out_bias_hbm, out_bias_ref),
                (gain_hbm, gain_ref),
                (shift_hbm, shift_ref),
            )
        )
    ]
    locals_ = [
        pltpu.make_async_copy(tokens_hbm.at[0], tok.at[me], local_sem.at[0]),
        pltpu.make_async_copy(weight_hbm, weight, local_sem.at[1]),
    ]
    for group, owner in enumerate((me, twin)):
        for at, (hbm, buf) in enumerate(((keys_hbm, kc), (values_hbm, vc))):
            locals_.append(
                pltpu.make_async_copy(
                    hbm.at[0, :, cols(owner, width)],
                    buf.at[group, core],
                    local_sem.at[2 + 2 * group + at],
                )
            )
    if gather:
        piece = out_weight_hbm.shape[1]
        out_copies = [
            pltpu.make_async_copy(out_weight_hbm, wo.at[0, :, cols(dp, piece)], local_sem.at[6])
        ]
    else:
        out_copies = [
            pltpu.make_async_copy(out_weight_hbm.at[owner], wo.at[at], local_sem.at[6 + at])
            for at, owner in enumerate((me, twin))
        ]

    def remote(src, dst, send, recv, device):
        return pltpu.make_async_remote_copy(
            src_ref=src,
            dst_ref=dst,
            send_sem=send,
            recv_sem=recv,
            device_id=device,
            device_id_type=MESH,
        )

    def near(src, dst, send, recv, index):
        return remote(src, dst, send, recv, {"seq": index})

    to_twin = near(tokens_hbm.at[0], tok.at[me], tok_send.at[1], tok_recv.at[1], twin)
    to_partner = near(tokens_hbm.at[0], tok.at[me], tok_send.at[0], tok_recv.at[0], partner)
    forward = near(tok.at[twin], tok.at[twin], tok_send.at[2], tok_recv.at[2], partner)
    cache_copies = []
    for group, owner in enumerate((partner, diag)):
        for at, (hbm, buf) in enumerate(((keys_hbm, kc), (values_hbm, vc))):
            cache_copies.append(
                near(
                    hbm.at[0, :, cols(owner, width)],
                    buf.at[group, core],
                    cache_send.at[2 * group + at],
                    cache_recv.at[2 * group + at],
                    partner,
                )
            )
    if gather:
        weight_twin = near(
            out_weight_hbm, wo.at[1, :, cols(dp, piece)], x_sem.at[0], x_sem.at[1], twin
        )
        z, y = dp // ROW, dp % ROW
        has_up, has_down = z < LINE - 1, z > 0
        above = jnp.minimum(dp + ROW, DP - 1)
        below = jnp.maximum(dp - ROW, 0)
        beside = dp + 1 - 2 * y

        def carry(part, slot, origin, device):
            at = wo.at[part, :, cols(origin, piece)]
            return remote(at, at, w_send.at[part, slot], w_recv.at[part, slot], {"dp": device})

        def up(part, j):
            return carry(part, j, jnp.maximum(dp - ROW * j, 0), above)

        def down(part, j):
            return carry(part, LINE - 1 + j, jnp.minimum(dp + ROW * j, DP - 1), below)

        def across(part, j):
            return carry(part, 2 * LINE - 2 + j, (dp + DP - ROW * j) % DP, beside)

        def skip(part):
            first = jnp.where(z == LINE - 1, y, dp)
            return carry(part, 3 * LINE - 2, dp, first)

        def step_up(part, j):
            @pl.when(z >= j)
            def _():
                up(part, j - 1).wait_recv()
                if j < LINE - 1:
                    pl.when(has_up)(lambda: up(part, j).start())
                across(part, j).start()

        def step_down(part, j):
            @pl.when(z + j < LINE)
            def _():
                if j < LINE - 1:
                    down(part, j - 1).wait_recv()
                else:
                    skip(part).wait_recv()
                if j < LINE - 2:
                    pl.when(has_down)(lambda: down(part, j).start())
                across(part, LINE - j).start()

        def begin_down(part):
            pl.when(has_down)(lambda: down(part, 0).start())
            pl.when(z == LINE - 1)(lambda: skip(part).start())
            pl.when(y == 1)(lambda: across(part, 0).start())

        def begin_up(part):
            pl.when(has_up)(lambda: up(part, 0).start())
            pl.when(y == 0)(lambda: across(part, 0).start())

    def steps(*moves):
        def move():
            for part, j, *way in moves:
                if way != [DOWN]:
                    step_up(part, j)
                if way != [UP]:
                    step_down(part, j)

        return move if gather else nothing

    barrier = pltpu.get_barrier_semaphore()

    def tell(sem, index):
        pl.semaphore_signal(sem, inc=1, device_id={"seq": index}, device_id_type=MESH)

    @pl.when(me == 1)
    def _():
        tell(barrier, 0)
        tell(barrier, 3)

    @pl.when(me == 3)
    def _():
        tell(barrier, 2)

    @pl.when(me != 1)
    def _():
        pl.semaphore_wait(barrier, 1 + (me == 2).astype(jnp.int32))

    @pl.when(me == 0)
    def _():
        tell(barrier, 2)
        tell(ready.at[0], 1)

    @pl.when(me == 2)
    def _():
        tell(ready.at[2], 0)
        tell(ready.at[2], 1)
        tell(ready.at[2], 3)

    @pl.when(me == 3)
    def _():
        tell(ready.at[3], 1)

    def cross():
        if gather:
            weight_twin.start()
        to_twin.start()

    @pl.when(chip == 1)
    def _():
        cross()

    for copy in locals_ + out_copies + small:
        copy.start()

    @pl.when(me == 1)
    def _():
        pl.semaphore_wait(ready.at[0], 1)

    @pl.when(me == 3)
    def _():
        pl.semaphore_wait(ready.at[2], 1)

    to_partner.start()
    for copy in cache_copies:
        copy.start()

    @pl.when(me == 0)
    def _():
        pl.semaphore_wait(ready.at[2], 1)

    @pl.when(me == 1)
    def _():
        pl.semaphore_wait(ready.at[3], 1)

    @pl.when(chip == 0)
    def _():
        cross()

    @pl.when(me == LEADER)
    def _():
        pl.semaphore_wait(ready.at[2], 1)

    def tell_far(sem, index):
        pl.semaphore_signal(sem, inc=1, device_id={"dp": index}, device_id_type=MESH)

    def spread_word(sem):
        @pl.when(me == LEADER)
        def _():
            for index in (0, 2, 3):
                tell(sem, index)

        @pl.when(me != LEADER)
        def _():
            pl.semaphore_wait(sem, 1)

    if gather:
        @pl.when(me == LEADER)
        def _():
            @pl.when(z + y > 0)
            def _():
                pl.semaphore_wait(barrier, has_down.astype(jnp.int32) + y)

            pl.when(has_up)(lambda: tell_far(barrier, above))
            pl.when(y == 0)(lambda: tell_far(barrier, beside))
            pl.when(has_down)(lambda: tell_far(up_sem.at[0], below))
            pl.when(y == 1)(lambda: tell_far(up_sem.at[1], beside))

        spread_word(far_ready.at[0])
        out_copies[0].wait()
        begin_down(0)

    def far_begin():
        @pl.when(me == LEADER)
        def _():
            pl.when(has_up)(lambda: pl.semaphore_wait(up_sem.at[0], 1))
            pl.when(y == 0)(lambda: pl.semaphore_wait(up_sem.at[1], 1))

        spread_word(far_ready.at[1])
        begin_up(0)

        @pl.when(z + y == 0)
        def _():
            weight_twin.wait_recv()

        begin_up(1)

    def far_early():
        @pl.when(z + y > 0)
        def _():
            weight_twin.wait_recv()
            begin_down(1)

    for copy in small:
        copy.wait()
    request = slot_ref[dp]
    cached = cached_ref[request]
    filled = span_ref[request]
    bias = bias_ref[:, cols(me, 3 * width)]
    low = lanes(rows) < HEAD_DIM
    ones = jnp.ones((rows, LANES), BF16)
    none = jnp.zeros((rows, LANES), BF16)

    def markers(count):
        lane = lanes(count)
        return (jnp.where(lane == at, 1.0, 0.0).astype(BF16) for at in (HEAD_DIM, 0))

    middle, first = markers(rows)

    def project(block):
        inputs = tok[block]
        side_, here_ = block // 2, rows_of(block % 2, rows)
        at = rows_of(old // rows + block, rows)
        for pair in range(heads // 2):
            here = slice(6 * pair * HEAD_DIM, 6 * (pair + 1) * HEAD_DIM)
            summed = jnp.dot(inputs, weight[:, here], preferred_element_type=F32) + bias[:, here]
            a, b, c = (summed[:, i * LANES : (i + 1) * LANES] for i in range(3))
            query = (jnp.where(low, a, b).astype(BF16).astype(F32) * HEAD_DIM**-0.5).astype(BF16)
            key = pltpu.roll(jnp.where(low, c, a), HEAD_DIM, 1).astype(BF16)
            value = jnp.where(low, b, c).astype(BF16)
            qo[block, :, pair * LANES : (pair + 1) * LANES] = query
            even, odd = split(query, middle, first)
            q0[side_, 2 * pair, here_], q0[side_, 2 * pair + 1, here_] = even, odd
            k0[2 * pair, at], k0[2 * pair + 1, at] = split(key, none, none)
            v0[2 * pair, at], v0[2 * pair + 1, at] = split(value, ones, ones)

    def query_copy(block):
        return near(qo.at[block], qt.at[block], q_send.at[block], q_recv.at[block], twin)

    def prepare(group, keys, values):
        lane_ = lanes(cache_rows)
        for c in range(2):
            place = lax.broadcasted_iota(jnp.int32, (cache_rows, LANES), 0)
            live = (2 * chip + c) * cache_rows + place < cached
            scale = jnp.where(live, 1.0, 0.0).astype(BF16)
            cap = jnp.where(live, 0.0, DEAD)
            cap_even = jnp.where(lane_ == HEAD_DIM, cap, 0.0).astype(BF16)
            cap_odd = jnp.where(lane_ == 0, cap, 0.0).astype(BF16)
            full = jnp.ones((cache_rows, LANES), BF16)
            at = slice(c * cache_rows, (c + 1) * cache_rows)
            for pair in range(heads // 2):
                here = slice(pair * LANES, (pair + 1) * LANES)
                key = kc[group, c, :, here] * scale
                keys[2 * pair, at], keys[2 * pair + 1, at] = split(key, cap_even, cap_odd)
                value = vc[group, c, :, here]
                values[2 * pair, at], values[2 * pair + 1, at] = split(value, full, full)

    def cached_keys(keys, values):
        return (lambda h: keys[h, 0:old]), (lambda h: values[h, 0:old])

    def new_keys(start, count):
        at = rows_of(old // half + start, half) if count == half else pl.ds(old, count)
        return (lambda h: k0[h, at]), (lambda h: v0[h, at])

    def own_heads(side_, fresh, cap, between=()):
        parts = [cached_keys(k0, v0), fresh]
        return attend(
            heads,
            lambda h: q0[side_, h],
            [k for k, _ in parts],
            [v for _, v in parts],
            [None, cap],
            between,
        )

    def twin_heads(side_, between=()):
        marks = list(markers(half))
        queries = []
        both = qt[pl.ds(2 * side_, 2)].reshape(half, width)
        for pair in range(heads // 2):
            queries.extend(split(both[:, pair * LANES : (pair + 1) * LANES], *marks))
        k, v = cached_keys(k1, v1)
        return attend(heads, lambda h: queries[h], [k], [v], [None], between)

    def part_copy(group, block):
        return near(
            part_send.at[group, block],
            part_recv.at[1 - group, block],
            p_send.at[group, block],
            p_recv.at[1 - group, block],
            twin,
        )

    def stat_copy(group):
        return near(
            stat_send.at[group],
            stat_recv.at[1 - group],
            s_sem.at[0, group],
            s_sem.at[1, 1 - group],
            twin,
        )

    locals_[0].wait()
    locals_[1].wait()
    project(me)
    to_partner.wait_recv()
    project(partner)

    row = lax.broadcasted_iota(jnp.int32, (half, half), 0)
    new = lax.broadcasted_iota(jnp.int32, (half, half), 1)
    near_cap[...] = jnp.where((new <= row) & (chip * half + new < filled), LIVE, DEAD)
    row = (1 - chip) * half + lax.broadcasted_iota(jnp.int32, (half, new_rows), 0)
    new = lax.broadcasted_iota(jnp.int32, (half, new_rows), 1)
    caps[...] = jnp.where((new <= row) & (new < filled), LIVE, DEAD)
    for at in (0, 1):
        locals_[2 + at].wait()
        cache_copies[at].wait_recv()
    prepare(0, k0, v0)
    query_copy(me).start()
    query_copy(partner).start()
    if gather:
        far_early()
    tops, products = own_heads(
        chip, new_keys(chip, half), near_cap[...], [nothing, far_begin if gather else nothing]
    )
    for h in range(heads):
        own_top[h] = jnp.broadcast_to(tops[h], (half, LANES))
        own_product[h] = products[h]
    for at in (2, 3):
        locals_[2 + at].wait()
        cache_copies[at].wait_recv()
    prepare(1, k1, v1)
    steps((0, 1), (1, 1))()

    to_twin.wait_recv()
    forward.start()
    project(twin)
    query_copy(twin).start()
    forward.wait_recv()
    project(diag)
    query_copy(diag).start()

    def send_part(group, tops, products):
        parts, stat = finish(tops, products)
        stat_send[group] = jnp.concatenate([stat[:rows].T[0:8], stat[rows:].T[0:8]], 1)
        stat_copy(group).start()
        for pair in range(heads // 2):
            both = parts[pair].astype(BF16)
            for block in range(2):
                part_send[group, block, :, pair * LANES : (pair + 1) * LANES] = both[
                    block * rows : (block + 1) * rows
                ]
        for block in (1 - core, core):
            part_copy(group, block).start()

    def keep_part(group, tops, products):
        parts, stat = finish(tops, products)
        for pair in range(heads // 2):
            at = slice(pair * LANES, (pair + 1) * LANES)
            keep[group, :, :, at] = parts[pair].reshape(2, rows, LANES)
        keep_stat[group] = stat

    query_copy(twin).wait_recv()
    query_copy(diag).wait_recv()
    send_part(1, *twin_heads(1 - chip, [steps((0, 2)), nothing, steps((1, 2), (0, 3, DOWN))]))
    send_part(0, *own_heads(1 - chip, new_keys(0, new_rows), caps[...]))
    steps((1, 3, DOWN), (0, 3, UP))()

    @pl.when(chip == 1)
    def _():
        fresh = lax.broadcasted_iota(jnp.int32, (1, half), 1) < filled
        k, v = new_keys(0, half)
        tops, products = attend(
            heads, lambda h: q0[1, h], [k], [v], [jnp.where(fresh, LIVE, DEAD)]
        )
        for h in range(heads):
            before = own_top[h]
            top = jnp.maximum(before, tops[h])
            own_product[h] = own_product[h] * jnp.exp(before - top) + products[h] * jnp.exp(
                tops[h] - top
            )
            own_top[h] = top

    keep_part(0, [own_top[h] for h in range(heads)], [own_product[h] for h in range(heads)])
    query_copy(me).wait_recv()
    query_copy(partner).wait_recv()
    keep_part(1, *twin_heads(chip, [nothing, steps((1, 3, UP))]))

    for copy in out_copies if not gather else []:
        copy.wait()
    def weights_there(part):
        if gather:
            for j in range(LINE):
                across(part, j).wait_recv()

    def weigh(group):
        stat_copy(1 - group).wait_recv()
        filler = jnp.zeros((LANES - 8, half), F32)
        other = jnp.concatenate([stat_recv[group], filler], 0).T
        share = 1.0 / (1.0 + jnp.exp(other - keep_stat[group]))
        wide = spread(share, heads).reshape(2, rows, width)
        keep[group] = keep[group] * wide
        rest[group] = 1.0 - wide

    def combine(group, block, at=slice(None)):
        attn = keep[group, block] + rest[group, block] * part_recv[group, block].astype(F32)
        return jnp.dot(attn.astype(BF16), wo[group, :, at], preferred_element_type=F32)

    model = wo.shape[2]
    sides = [slice(i * model // 2, (i + 1) * model // 2) for i in range(2)]
    mixed_copies = [
        near(mixed_send.at[:, at], mixed_recv.at[:, at], m_sem.at[0, i], m_sem.at[1, i], partner)
        for i, at in enumerate(sides)
    ]
    weigh(0)
    weights_there(0)
    for block in range(2):
        part_copy(1, block).wait_recv()
        mixed_sum[block] = combine(0, block)
    mixed_sum[core] = mixed_sum[core] + out_bias_ref[...] + tok[me].astype(F32)
    weigh(1)
    sent = [to_partner, to_twin, forward, stat_copy(0), stat_copy(1)] + cache_copies
    sent += [query_copy(b) for b in range(tok.shape[0])]
    sent += [part_copy(1, b) for b in range(2)]
    if gather:
        sent += [weight_twin] + [across(0, j) for j in range(LINE)]
        for part in range(2):
            for j in range(LINE - 1):
                pl.when(has_up & (z >= j))(up(part, j).wait_send)
                if j < LINE - 2:
                    pl.when(has_down & (z + j < LINE))(down(part, j).wait_send)
            pl.when(z == LINE - 1)(skip(part).wait_send)
    for copy in sent:
        copy.wait_send()
    weights_there(1)
    part_copy(0, 1 - core).wait_recv()
    for at, copy in zip(sides, mixed_copies):
        mixed_send[:, at] = (mixed_sum[1 - core, :, at] + combine(1, 1 - core, at)).astype(BF16)
        copy.start()
    part_copy(0, core).wait_recv()
    mixed = mixed_sum[core] + combine(1, core)
    for copy in mixed_copies:
        copy.wait_recv()
    mixed = mixed + mixed_recv[...].astype(F32)
    center = mixed - jnp.mean(mixed, axis=1, keepdims=True)
    variance = jnp.mean(center * center, axis=1, keepdims=True)
    normed = center * lax.rsqrt(variance + 1e-05) * gain_ref[...] + shift_ref[...]
    out_ref[0] = normed.astype(BF16)

    last = [part_copy(0, b) for b in range(2)] + mixed_copies
    if gather:
        last += [across(1, j) for j in range(LINE)]
    for copy in last:
        copy.wait_send()


def local(
    tokens,
    cache_keys,
    cache_values,
    qkv_weight,
    qkv_bias,
    out_weight,
    out_bias,
    norm_gain,
    norm_bias,
    cached_len,
    span_len,
    slot_request,
):
    rows, model = tokens.shape[1:]
    cache_rows = cache_keys.shape[1]
    width = qkv_weight.shape[1] // 3
    heads = width // HEAD_DIM
    blocks = lax.axis_size("seq")
    half = 2 * rows
    old = 2 * cache_rows
    total = old + blocks * rows
    hbm = pl.BlockSpec(memory_space=pltpu.HBM)
    vmem = pl.BlockSpec(memory_space=pltpu.VMEM)
    dma = pltpu.SemaphoreType.DMA

    gather = lax.axis_size("dp") == DP and out_weight.shape[1] % 128 == 0
    if not gather:
        out_weight = lax.all_gather(out_weight, "dp", axis=1, tiled=True)
        out_weight = lax.all_gather(out_weight, "seq", axis=0)

    return pl.pallas_call(
        functools.partial(kernel, gather),
        out_shape=pltpu.VMEM((1, rows, model), BF16),
        in_specs=[hbm] * 12,
        out_specs=vmem,
        scratch_shapes=[
            pltpu.SMEM(cached_len.shape, jnp.int32),
            pltpu.SMEM(span_len.shape, jnp.int32),
            pltpu.SMEM(slot_request.shape, jnp.int32),
            pltpu.VMEM((1, qkv_bias.size), F32),
            pltpu.VMEM((1, model), F32),
            pltpu.VMEM((1, model), F32),
            pltpu.VMEM((1, model), F32),
            dma((7,)),
            pltpu.VMEM((blocks, rows, model), BF16),
            pltpu.VMEM((model, 3 * width), BF16),
            pltpu.VMEM((2, 2, cache_rows, width), BF16),
            pltpu.VMEM((2, 2, cache_rows, width), BF16),
            pltpu.VMEM((heads, total, LANES), BF16),
            pltpu.VMEM((heads, total, LANES), BF16),
            pltpu.VMEM((heads, old, LANES), BF16),
            pltpu.VMEM((heads, old, LANES), BF16),
            pltpu.VMEM((2, heads, half, LANES), BF16),
            pltpu.VMEM((blocks, rows, width), BF16),
            pltpu.VMEM((blocks, rows, width), BF16),
            pltpu.VMEM((half, half), F32),
            pltpu.VMEM((half, blocks * rows), F32),
            pltpu.VMEM((heads, half, LANES), F32),
            pltpu.VMEM((heads, half, LANES), F32),
            pltpu.VMEM((2, 2, rows, width), F32),
            pltpu.VMEM((2, half, LANES), F32),
            pltpu.VMEM((2, 2, rows, width), F32),
            pltpu.VMEM((2, rows, model), F32),
            pltpu.VMEM((2, 2, rows, width), BF16),
            pltpu.VMEM((2, 2, rows, width), BF16),
            pltpu.VMEM((2, 8, half), F32),
            pltpu.VMEM((2, 8, half), F32),
            pltpu.VMEM((rows, model), BF16),
            pltpu.VMEM((rows, model), BF16),
            pltpu.VMEM((2, width, model), BF16),
            dma((8,)),
            dma((3,)),
            dma((3,)),
            dma((4,)),
            dma((4,)),
            dma((blocks,)),
            dma((blocks,)),
            dma((2, 2)),
            dma((2, 2)),
            dma((2, 2)),
            dma((2, 2)),
            dma((2,)),
            dma((2, 3 * LINE - 1)),
            dma((2, 3 * LINE - 1)),
            pltpu.SemaphoreType.REGULAR((4,)),
            pltpu.SemaphoreType.REGULAR((2,)),
            pltpu.SemaphoreType.REGULAR((2,)),
        ],
        compiler_params=pltpu.CompilerParams(
            collective_id=0, has_side_effects=True, vmem_limit_bytes=60 << 20
        ),
        cost_estimate=pl.CostEstimate(
            flops=6_000_000_000, bytes_accessed=6_000_000, transcendentals=5_000_000
        ),
        name="sublayer",
    )(
        cached_len,
        span_len,
        slot_request,
        tokens,
        cache_keys,
        cache_values,
        qkv_weight,
        out_weight,
        qkv_bias.reshape(1, -1),
        out_bias.reshape(1, -1),
        norm_gain.reshape(1, -1),
        norm_bias.reshape(1, -1),
    )


def solution(mesh):
    return jax.shard_map(
        local,
        mesh=mesh,
        in_specs=(
            P("dp", "seq", None),
            P("dp", "seq", None),
            P("dp", "seq", None),
            P(None, "seq"),
            P(),
            P("seq", "dp"),
            P(),
            P(),
            P(),
            P(),
            P(),
            P(),
        ),
        out_specs=P("dp", "seq", None),
        check_vma=False,
    )
```
